128 devices in a mesh: grp: 2 (over z_hi), pix: 64 (over x, y, z_lo, core).
Axes of the slice: x: 4, y: 4, z: 4 (z_hi: 2, z_lo: 2; z = z_hi * 2 + z_lo), core: 2. Of those that a mesh axis runs over, the one named last changes fastest.
Arguments:
- fields: bfloat16 [2, 2, 128, 512, 512], P('grp', None, None, 'pix'), may hold values from -6 to 6
- lens_phase: float32 [512, 512], P('pix'), may hold values from -3.140625 to 3.140625
- occupancy: float32 [256], replicated, may hold values from 0.05 to 1
- focus_scale: float32 [256], replicated, may hold values from 0.5 to 1.5
- assignment: int32 [256], replicated, may hold values from 0 to 255, each once
- start_basis: float32 [2, 256, 128], replicated, may hold values from -6 to 6
Outputs:
- coherent_modes: bfloat16 [2, 128, 512, 512], P(None, None, 'pix', 'grp')
- relative_power: float32 [128], replicated
The draws below stay inside these ranges and needn't reach their ends.
Inputs may be any that keep to these rules, and one draw needn't show every extreme that they name: `assignment`: each electron is carried by exactly one wavefront slot.
All inputs are finite; a program needn't handle non-finite values.
Results may differ from the reference program's by a relative error of at most 0.0018.
The reference program's roundings to bfloat16 on the way count: a program that leaves them out, or rounds other values in their place, can miss the bound.
Values may be sent and summed in bfloat16 or wider, within the bound.
No kernel may reach another device: no remote copies, remote signals or barrier semaphores. Data moves between devices by JAX's collectives and lax.ppermute only.
A program may use at most 64 MiB of HBM per device.

```python
import math
import jax
import jax.numpy as jnp
from jax import lax

NROW = 512
NCOL = 512
MODES = 128
RANK = 128
STEPS = 2
STACK = 256
ELECTRONS = 256
N_GRP = 2


def draw_fields(key, part):
    shared_count = 32
    key_shared = jax.random.fold_in(key, 11)
    key_coeff = jax.random.fold_in(key, 12)
    key_noise = jax.random.fold_in(key, 13)
    decay = 0.8
    shared = jax.random.normal(key_shared, (2, shared_count, NROW * NCOL), jnp.float32)
    noise_level = 0.3
    order = jnp.arange(shared_count, dtype=jnp.float32)
    weights = decay ** order
    coeff = jax.random.normal(key_coeff, (2, N_GRP * MODES, shared_count), jnp.float32) * weights[None, None, :] * 0.70710678
    mixed_re = jnp.dot(coeff[0], shared[0]) - jnp.dot(coeff[1], shared[1])
    mixed_im = jnp.dot(coeff[0], shared[1]) + jnp.dot(coeff[1], shared[0])
    noise = jax.random.normal(key_noise, (2, N_GRP * MODES, NROW * NCOL), jnp.float32)
    total = jnp.sum(weights * weights)
    norm = 1.0 / jnp.sqrt(total + noise_level * noise_level)
    values = (jnp.stack([mixed_re, mixed_im]) + noise_level * noise) * norm
    values = jnp.clip(values, -6.0, 6.0)
    values = values.reshape(2, N_GRP, MODES, NROW, NCOL)
    return jnp.swapaxes(values, 0, 1).astype(jnp.bfloat16)


def normal_values(rng, shape, scale, limit, kind=jnp.bfloat16):
    return jnp.clip(scale * jax.random.normal(rng, shape, jnp.float32), -limit, limit).astype(kind)


def setup_inputs(seed: int = 0) -> dict:
    key_list = jax.random.split(jax.random.key(seed), 7)
    fields = draw_fields(jax.random.fold_in(key_list[6], 71), 0)
    lens_phase = jnp.clip(jax.random.uniform(key_list[1], (NROW, NCOL), jnp.float32, -3.140625, 3.140625), -3.140625, 3.140625)
    occupancy = jnp.clip(jnp.exp(jax.random.uniform(key_list[2], (ELECTRONS,), jnp.float32, math.log(0.05), math.log(1.0))), 0.05, 1.0)
    focus_scale = jnp.clip(jax.random.uniform(key_list[3], (ELECTRONS,), jnp.float32, 0.5, 1.5), 0.5, 1.5)
    assignment = jax.random.permutation(key_list[4], ELECTRONS).astype(jnp.int32)
    start_basis = normal_values(key_list[5], (2, STACK, RANK), 1.0, 6.0, jnp.float32)
    return dict(fields=fields, lens_phase=lens_phase, occupancy=occupancy, focus_scale=focus_scale, assignment=assignment, start_basis=start_basis)


def dft_tables(length):
    index = jnp.arange(length, dtype=jnp.int32)
    product = index[:, None] * index[None, :] % length
    angle = product.astype(jnp.float32) * (2.0 * math.pi / length)
    factor = 1.0 / math.sqrt(length)
    return ((jnp.cos(angle) * factor).astype(jnp.bfloat16), (jnp.sin(angle) * factor).astype(jnp.bfloat16))

def transform_last(stacked, cosine, sine):
    values = stacked.astype(jnp.float32)
    with_cos = jnp.dot(values, cosine.astype(jnp.float32), precision=lax.Precision.HIGHEST)
    with_sin = jnp.dot(values, sine.astype(jnp.float32), precision=lax.Precision.HIGHEST)
    real_part = with_cos[0] + with_sin[1]
    imag_part = with_cos[1] - with_sin[0]
    return jnp.stack([real_part, imag_part]).astype(jnp.bfloat16)

def reference(fields, lens_phase, occupancy, focus_scale, assignment, start_basis):
    highest = lax.Precision.HIGHEST
    cos_cols, sin_cols = dft_tables(NCOL)
    cos_rows, sin_rows = dft_tables(NROW)
    stacks = []
    for group_index in range(N_GRP):
        electron = assignment[group_index * MODES:(group_index + 1) * MODES]
        amplitude = jnp.sqrt(occupancy[electron])[:, None, None]
        angle = focus_scale[electron][:, None, None] * lens_phase[None]
        cosine = jnp.cos(angle)
        sine = jnp.sin(angle)
        field_re = fields[group_index, 0].astype(jnp.float32)
        field_im = fields[group_index, 1].astype(jnp.float32)
        phased = jnp.stack([amplitude * (field_re * cosine - field_im * sine), amplitude * (field_re * sine + field_im * cosine)]).astype(jnp.bfloat16)
        across = transform_last(phased, cos_cols, sin_cols)
        across = jnp.swapaxes(across, 2, 3)
        stacks.append(transform_last(across, cos_rows, sin_rows))
    stack = jnp.concatenate(stacks, axis=1)
    flat = stack.reshape(2, STACK, NCOL * NROW).astype(jnp.float32)
    gram_re = jnp.dot(flat[0], flat[0].T, precision=highest) + jnp.dot(flat[1], flat[1].T, precision=highest)
    gram_im = jnp.dot(flat[0], flat[1].T, precision=highest) - jnp.dot(flat[1], flat[0].T, precision=highest)
    basis_re = start_basis[0]
    basis_im = start_basis[1]
    for iteration in range(STEPS):
        image_re = jnp.dot(gram_re, basis_re, precision=highest) - jnp.dot(gram_im, basis_im, precision=highest)
        image_im = jnp.dot(gram_re, basis_im, precision=highest) + jnp.dot(gram_im, basis_re, precision=highest)
        column_norm = jnp.sqrt(lax.optimization_barrier(jnp.sum(image_re * image_re + image_im * image_im, axis=0)) + 1e-06)
        basis_re = image_re / column_norm[None, :]
        basis_im = image_im / column_norm[None, :]
    rounded = jnp.stack([basis_re, basis_im]).astype(jnp.bfloat16).astype(jnp.float32)
    mode_re = jnp.dot(rounded[0].T, flat[0], precision=highest) - jnp.dot(rounded[1].T, flat[1], precision=highest)
    mode_im = jnp.dot(rounded[0].T, flat[1], precision=highest) + jnp.dot(rounded[1].T, flat[0], precision=highest)
    energy = lax.optimization_barrier(jnp.sum(mode_re * mode_re + mode_im * mode_im, axis=1))
    trace = jnp.sum(jnp.diagonal(gram_re))
    relative_power = energy * STACK / trace
    inverse = lax.rsqrt(energy / (NROW * NCOL) + 1e-06)
    coherent_modes = (jnp.stack([mode_re, mode_im]) * inverse[None, :, None]).astype(jnp.bfloat16)
    return (coherent_modes.reshape(2, RANK, NCOL, NROW), relative_power)
```

```python
import math

import jax
import jax.numpy as jnp
import numpy as np
from jax import lax
from jax.experimental import pallas as pl
from jax.experimental.pallas import tpu as pltpu
from jax.sharding import PartitionSpec as P

NROW = 512
NCOL = 512
STEPS = 2
GROUPS = 2
PIX = 64
DEVICES = GROUPS * PIX
SLOTS = 128
STACK = GROUPS * SLOTS
RANK = 128
ROWS = NROW // PIX
COLS = NCOL // DEVICES
HALF = NROW // GROUPS
WIDE = RANK * GROUPS * COLS
AXES = ("grp", "pix")

PI_HI = 3.140625
PI_LO = math.pi - 3.140625


def fit(function, terms):
    limit = (math.pi / 2) * 1.001
    nodes = np.cos(np.pi * (np.arange(400) + 0.5) / 400)
    square = (nodes + 1.0) * 0.5 * limit * limit
    powers = np.stack([square**k for k in range(terms)], axis=1)
    return [float(c) for c in np.linalg.lstsq(powers, function(np.sqrt(square)), rcond=None)[0]]


SIN_FIT = fit(lambda x: np.sin(x) / x, 5)
COS_FIT = fit(np.cos, 6)


def tables(length):
    index = np.arange(length, dtype=np.int64)
    angle = (index[:, None] * index[None, :] % length).astype(np.float32) * np.float32(
        2.0 * math.pi / length
    )
    factor = np.float32(1.0 / math.sqrt(length))
    cosine = (np.cos(angle) * factor).astype(jnp.bfloat16)
    sine = (np.sin(angle) * factor).astype(jnp.bfloat16)
    return cosine, sine


def column_tables():
    i, g, p = np.meshgrid(np.arange(COLS), np.arange(GROUPS), np.arange(PIX), indexing="ij")
    order = (p * (GROUPS * COLS) + g * COLS + i).reshape(-1)
    cosine, sine = tables(NCOL)
    return cosine[order], sine[order]


def row_tables():
    cosine, sine = tables(NROW)
    cosine = cosine.reshape(NROW, PIX, ROWS)
    sine = sine.reshape(NROW, PIX, ROWS)
    real = np.stack([cosine, sine], axis=2).reshape(NROW, 2 * NROW)
    imag = np.stack([-sine, cosine], axis=2).reshape(NROW, 2 * NROW)
    return np.concatenate([real, imag], axis=0)


def polynomial(square, coefficients):
    total = square * coefficients[-1] + coefficients[-2]
    for coefficient in coefficients[-3::-1]:
        total = total * square + coefficient
    return total


def spectra_kernel(
    group_ref, assign_ref, occ_ref, chrom_ref, fields_ref, lens_ref, cos_ref, sin_ref, out_ref,
    real_ref, imag_ref, wide_ref,
):
    base = group_ref[0] * SLOTS

    def phase(m, carry):
        electron = assign_ref[base + m]
        amplitude = jnp.sqrt(jnp.full((ROWS, 128), occ_ref[electron], jnp.float32))
        chromatic = chrom_ref[electron]
        for lane in range(NCOL // 128):
            cut = pl.ds(lane * 128, 128)
            angle = lens_ref[:, cut] * chromatic
            turns = jnp.round(angle * (1.0 / math.pi))
            rest = (angle - turns * PI_HI) - turns * PI_LO
            square = rest * rest
            signed = amplitude * (1.0 - 2.0 * (turns * turns))
            sine = signed * (rest * polynomial(square, SIN_FIT))
            cosine = signed * polynomial(square, COS_FIT)
            field_re = fields_ref[0, m, :, cut].astype(jnp.float32)
            field_im = fields_ref[1, m, :, cut].astype(jnp.float32)
            rows = pl.ds(lane * ROWS * SLOTS + m, ROWS, stride=SLOTS)
            real_ref[rows, :] = field_re * cosine - field_im * sine
            imag_ref[rows, :] = field_re * sine + field_im * cosine
        return carry

    lax.fori_loop(0, SLOTS, phase, 0, unroll=2)
    contract = (((1,), (1,)), ((), ()))

    def product(table, wave):
        return lax.dot_general(table, wave, contract, preferred_element_type=jnp.float32)

    def wave(ref, j):
        lanes = [
            ref[pl.ds((lane * ROWS + j) * SLOTS, 2 * SLOTS), :] for lane in range(NCOL // 128)
        ]
        return jnp.concatenate(lanes, axis=1).astype(jnp.bfloat16)

    def spectrum(i, carry):
        rows = pl.ds(pl.multiple_of(i * DEVICES, DEVICES), DEVICES)
        cosine = cos_ref[rows, :]
        sine = sin_ref[rows, :]
        for j in range(0, ROWS, 2):
            wave_re = wave(real_ref, j)
            wave_im = wave(imag_ref, j)
            across_re = product(cosine, wave_re) + product(sine, wave_im)
            across_im = product(cosine, wave_im) - product(sine, wave_re)
            for part, across in ((0, across_re), (1, across_im)):
                for q in range(2):
                    at = part * ROWS + j + q
                    wide_ref[pl.ds(at, DEVICES, stride=2 * ROWS), :] = across[
                        :, q * SLOTS : (q + 1) * SLOTS
                    ]
        out_ref[:, i] = wide_ref[...].astype(jnp.bfloat16).reshape(DEVICES, 2 * ROWS, SLOTS)
        return carry

    lax.fori_loop(0, COLS, spectrum, 0)


def focal_kernel(group_ref, pieces_ref, table_ref, keep_ref, send_ref, gram_ref):
    group = group_ref[0]
    real = jnp.zeros((STACK, STACK), jnp.float32)
    cross = jnp.zeros((STACK, STACK), jnp.float32)
    for i in range(COLS):
        wave = jnp.concatenate(
            [
                pieces_ref[g * PIX : (g + 1) * PIX, i].reshape(2 * NROW, SLOTS)
                for g in range(GROUPS)
            ],
            axis=1,
        )
        focal = [
            jnp.dot(
                table_ref[part * NROW : (part + 1) * NROW, :],
                wave,
                preferred_element_type=jnp.float32,
            ).astype(jnp.bfloat16)
            for part in range(2)
        ]
        turned = [focal[part].T for part in range(2)]
        for part in range(2):
            low, high = turned[part][:, :HALF], turned[part][:, HALF:]
            keep_ref[part, i] = jnp.where(group == 0, low, high)
            send_ref[part, i] = jnp.where(group == 0, high, low)
        real += jnp.dot(turned[0], focal[0], preferred_element_type=jnp.float32)
        real += jnp.dot(turned[1], focal[1], preferred_element_type=jnp.float32)
        cross += jnp.dot(turned[0], focal[1], preferred_element_type=jnp.float32)
    imag = cross - cross.T
    row = lax.broadcasted_iota(jnp.int32, (STACK, STACK), 0)
    column = lax.broadcasted_iota(jnp.int32, (STACK, STACK), 1)
    packed = jnp.where(row <= column, real, imag)
    for q in range(4):
        top, left = (q // 2) * 128, (q % 2) * 128
        gram_ref[pl.ds(q, 128, stride=4), :] = packed[top : top + 128, left : left + 128]


def total_kernel(parts_ref, out_ref):
    total = jnp.sum(parts_ref[...].reshape(DEVICES // 2, 8, 128), axis=0)
    total = total[:4] + total[4:]
    twice = jnp.concatenate([total, total], axis=0)
    out_ref[...] = jnp.broadcast_to(twice[None], (DEVICES // 2, 8, 128)).reshape(4 * DEVICES, 128)


def modes_kernel(group_ref, gram_ref, start_ref, keep_ref, other_ref, out_ref, power_ref, wide_ref):
    highest = lax.Precision.HIGHEST
    quads = [gram_ref[pl.ds(q, 128, stride=4), :] for q in range(4)]
    packed = jnp.concatenate(
        [jnp.concatenate(quads[:2], axis=1), jnp.concatenate(quads[2:], axis=1)], axis=0
    )
    turned = packed.T
    row = lax.broadcasted_iota(jnp.int32, (STACK, STACK), 0)
    column = lax.broadcasted_iota(jnp.int32, (STACK, STACK), 1)
    gram_re = jnp.where(row <= column, packed, turned)
    gram_im = jnp.where(row > column, packed, jnp.where(row == column, 0.0, -turned))

    def product(a, b):
        return jnp.dot(a, b, precision=highest, preferred_element_type=jnp.float32)

    def apply(re, im):
        return (
            product(gram_re, re) - product(gram_im, im),
            product(gram_re, im) + product(gram_im, re),
        )

    basis_re, basis_im = start_ref[0], start_ref[1]
    for _ in range(STEPS):
        image_re, image_im = apply(basis_re, basis_im)
        norm = jnp.sqrt(
            jnp.sum(image_re * image_re + image_im * image_im, axis=0, keepdims=True) + 1e-06
        )
        basis_re = image_re / norm
        basis_im = image_im / norm
    rounded_re = basis_re.astype(jnp.bfloat16)
    rounded_im = basis_im.astype(jnp.bfloat16)
    wide_re = rounded_re.astype(jnp.float32)
    wide_im = rounded_im.astype(jnp.float32)
    image_re, image_im = apply(wide_re, wide_im)
    energy = jnp.sum(wide_re * image_re + wide_im * image_im, axis=0, keepdims=True)
    trace = jnp.sum(jnp.where(row == column, packed, 0.0))
    power_ref[...] = energy * STACK / trace
    inverse = lax.rsqrt(energy / (NROW * NCOL) + 1e-06)
    scale = jnp.broadcast_to(inverse, (RANK, RANK)).T
    left_re = wide_re.T.astype(jnp.bfloat16)
    left_im = wide_im.T.astype(jnp.bfloat16)
    group = group_ref[0]

    def multiply(a, b):
        return jnp.dot(a, b, preferred_element_type=jnp.float32)

    for part in range(2):
        for source, ref in ((0, keep_ref), (1, other_ref)):
            first = jnp.where(group == source, 0, COLS)
            for i in range(COLS):
                focal_re, focal_im = ref[0, i], ref[1, i]
                if part == 0:
                    mode = multiply(left_re, focal_re) - multiply(left_im, focal_im)
                else:
                    mode = multiply(left_re, focal_im) + multiply(left_im, focal_re)
                for lane in range(HALF // 128):
                    rows = pl.ds(lane * WIDE + first + i, RANK, stride=GROUPS * COLS)
                    wide_ref[rows, :] = mode[:, lane * 128 : (lane + 1) * 128] * scale
        for lane in range(HALF // 128):
            out_ref[part, :, :, lane * 128 : (lane + 1) * 128] = (
                wide_ref[lane * WIDE : (lane + 1) * WIDE, :]
                .reshape(RANK, GROUPS * COLS, 128)
                .astype(jnp.bfloat16)
            )


VMEM = pl.BlockSpec(memory_space=pltpu.VMEM)
SMEM = pl.BlockSpec(memory_space=pltpu.SMEM)
PARAMS = pltpu.CompilerParams(vmem_limit_bytes=56 * 1024 * 1024)


def local(fields, lens_phase, occupancy, focus_scale, assignment, start_basis):
    group = lax.axis_index("grp").astype(jnp.int32).reshape(1)
    cos_cols, sin_cols = (jnp.asarray(table) for table in column_tables())
    across = pl.pallas_call(
        spectra_kernel,
        out_shape=jax.ShapeDtypeStruct((DEVICES, COLS, 2 * ROWS, SLOTS), jnp.bfloat16),
        in_specs=[SMEM] * 4 + [VMEM] * 4,
        out_specs=VMEM,
        scratch_shapes=[
            pltpu.VMEM((NCOL // 128 * ROWS * SLOTS, 128), jnp.float32),
            pltpu.VMEM((NCOL // 128 * ROWS * SLOTS, 128), jnp.float32),
            pltpu.VMEM((DEVICES * 2 * ROWS, SLOTS), jnp.float32),
        ],
        compiler_params=PARAMS,
        name="spectra",
    )(group, assignment, occupancy, focus_scale, fields[0], lens_phase, cos_cols, sin_cols)
    pieces = lax.all_to_all(across, AXES, 0, 0, tiled=True)
    focal_shape = jax.ShapeDtypeStruct((2, COLS, STACK, HALF), jnp.bfloat16)
    keep, send, gram = pl.pallas_call(
        focal_kernel,
        out_shape=(
            focal_shape,
            focal_shape,
            jax.ShapeDtypeStruct((4 * DEVICES, 128), jnp.float32),
        ),
        in_specs=[SMEM] + [VMEM] * 2,
        out_specs=(VMEM,) * 3,
        compiler_params=PARAMS,
        name="focal",
    )(group, pieces, jnp.asarray(row_tables()))
    other = lax.ppermute(send, "grp", [(0, 1), (1, 0)])
    parts = lax.all_to_all(gram.reshape(DEVICES, 4, 128), AXES, 0, 0, tiled=True)
    total = pl.pallas_call(
        total_kernel,
        out_shape=jax.ShapeDtypeStruct((4 * DEVICES, 128), jnp.float32),
        in_specs=[VMEM],
        out_specs=VMEM,
        compiler_params=PARAMS,
        name="total",
    )(parts.reshape(4 * DEVICES, 128))
    whole = lax.all_to_all(total.reshape(DEVICES, 4, 128), AXES, 0, 0, tiled=True)
    coherent_modes, power = pl.pallas_call(
        modes_kernel,
        out_shape=(
            jax.ShapeDtypeStruct((2, RANK, GROUPS * COLS, HALF), jnp.bfloat16),
            jax.ShapeDtypeStruct((1, RANK), jnp.float32),
        ),
        in_specs=[SMEM] + [VMEM] * 4,
        out_specs=(VMEM,) * 2,
        scratch_shapes=[pltpu.VMEM((HALF // 128 * WIDE, 128), jnp.float32)],
        compiler_params=PARAMS,
        name="modes",
    )(group, whole.reshape(4 * DEVICES, 128), start_basis, keep, other)
    return coherent_modes, power.reshape(RANK)


def solution(mesh):
    in_specs = (P("grp", None, None, "pix", None), P("pix", None), P(), P(), P(), P())
    out_specs = (P(None, None, "pix", "grp"), P())
    return jax.shard_map(local, mesh=mesh, in_specs=in_specs, out_specs=out_specs, check_vma=False)
```

```python
import math

import jax
import jax.numpy as jnp
import numpy as np
from jax import lax
from jax.experimental import pallas as pl
from jax.experimental.pallas import tpu as pltpu
from jax.sharding import PartitionSpec as P

NROW = 512
NCOL = 512
STEPS = 2
GROUPS = 2
PIX = 64
DEVICES = GROUPS * PIX
SLOTS = 128
STACK = GROUPS * SLOTS
RANK = 128
ROWS = NROW // PIX
COLS = NCOL // DEVICES
HALF = NROW // GROUPS
WIDE = RANK * GROUPS * COLS
BLOCK = DEVICES * 2 * ROWS
AXES = ("grp", "pix")

LIMIT = 0.5 * 1.5 * 3.140625


def fit(function, terms):
    limit = LIMIT * 1.001
    nodes = np.cos(np.pi * (np.arange(400) + 0.5) / 400)
    square = (nodes + 1.0) * 0.5 * limit * limit
    powers = np.stack([square**k for k in range(terms)], axis=1)
    return [float(c) for c in np.linalg.lstsq(powers, function(np.sqrt(square)), rcond=None)[0]]


SIN_FIT = fit(lambda x: np.sin(x) / x, 6)
COS_FIT = fit(np.cos, 7)


def tables(length):
    index = np.arange(length, dtype=np.int64)
    angle = (index[:, None] * index[None, :] % length).astype(np.float32) * np.float32(
        2.0 * math.pi / length
    )
    factor = np.float32(1.0 / math.sqrt(length))
    cosine = (np.cos(angle) * factor).astype(jnp.bfloat16)
    sine = (np.sin(angle) * factor).astype(jnp.bfloat16)
    return cosine, sine


def column_tables():
    i, g, p = np.meshgrid(np.arange(COLS), np.arange(GROUPS), np.arange(PIX), indexing="ij")
    order = (p * (GROUPS * COLS) + g * COLS + i).reshape(-1)
    cosine, sine = tables(NCOL)
    return cosine[order], sine[order]


def row_tables():
    cosine, sine = tables(NROW)
    cosine = cosine.reshape(NROW, PIX, ROWS)
    sine = sine.reshape(NROW, PIX, ROWS)
    real = np.stack([cosine, sine], axis=2).reshape(NROW, 2 * NROW)
    imag = np.stack([-sine, cosine], axis=2).reshape(NROW, 2 * NROW)
    return np.concatenate([real, imag], axis=0)


def polynomial(square, coefficients):
    total = square * coefficients[-1] + coefficients[-2]
    for coefficient in coefficients[-3::-1]:
        total = total * square + coefficient
    return total


def spectra_kernel(
    group_ref, assign_ref, occ_ref, chrom_ref, fields_ref, lens_ref, cos_ref, sin_ref, out_ref,
    real_ref, imag_ref, wide_ref,
):
    base = group_ref[0] * SLOTS

    def phase(m, carry):
        electron = assign_ref[base + m]
        amplitude = jnp.sqrt(jnp.full((ROWS, 128), occ_ref[electron], jnp.float32))
        twice = amplitude + amplitude
        chromatic = chrom_ref[electron] * 0.5
        for lane in range(NCOL // 128):
            cut = pl.ds(lane * 128, 128)
            half = lens_ref[:, cut] * chromatic
            square = half * half
            sine_half = half * polynomial(square, SIN_FIT)
            scaled = sine_half * twice
            sine = scaled * polynomial(square, COS_FIT)
            cosine = amplitude - scaled * sine_half
            field_re = fields_ref[0, m, :, cut].astype(jnp.float32)
            field_im = fields_ref[1, m, :, cut].astype(jnp.float32)
            rows = pl.ds(pl.multiple_of(lane * ROWS * SLOTS + m * ROWS, ROWS), ROWS)
            real_ref[rows, :] = field_re * cosine - field_im * sine
            imag_ref[rows, :] = field_re * sine + field_im * cosine
        return carry

    lax.fori_loop(0, SLOTS, phase, 0, unroll=4)
    contract = (((1,), (1,)), ((), ()))

    def product(table, wave):
        return lax.dot_general(table, wave, contract, preferred_element_type=jnp.float32)

    def wave(ref, j):
        return jnp.concatenate(
            [
                jnp.concatenate(
                    [
                        ref[pl.ds(lane * ROWS * SLOTS + j + q, SLOTS, stride=ROWS), :]
                        for lane in range(NCOL // 128)
                    ],
                    axis=1,
                )
                for q in range(2)
            ],
            axis=0,
        ).astype(jnp.bfloat16)

    cosine = cos_ref[...]
    sine = sin_ref[...]
    for j in range(0, ROWS, 2):
        wave_re = wave(real_ref, j)
        wave_im = wave(imag_ref, j)
        across_re = product(cosine, wave_re) + product(sine, wave_im)
        across_im = product(cosine, wave_im) - product(sine, wave_re)
        for part, across in ((0, across_re), (1, across_im)):
            for q in range(2):
                for i in range(COLS):
                    at = i * BLOCK + part * ROWS + j + q
                    wide_ref[pl.ds(at, DEVICES, stride=2 * ROWS), :] = across[
                        i * DEVICES : (i + 1) * DEVICES, q * SLOTS : (q + 1) * SLOTS
                    ]
    for i in range(COLS):
        out_ref[:, i] = (
            wide_ref[i * BLOCK : (i + 1) * BLOCK, :]
            .astype(jnp.bfloat16)
            .reshape(DEVICES, 2 * ROWS, SLOTS)
        )


def focal_kernel(group_ref, pieces_ref, table_ref, keep_ref, send_ref, gram_ref):
    group = group_ref[0]
    real = jnp.zeros((STACK, STACK), jnp.float32)
    cross = jnp.zeros((STACK, STACK), jnp.float32)
    for i in range(COLS):
        wave = jnp.concatenate(
            [
                pieces_ref[g * PIX : (g + 1) * PIX, i].reshape(2 * NROW, SLOTS)
                for g in range(GROUPS)
            ],
            axis=1,
        )
        focal = [
            jnp.dot(
                table_ref[part * NROW : (part + 1) * NROW, :],
                wave,
                preferred_element_type=jnp.float32,
            ).astype(jnp.bfloat16)
            for part in range(2)
        ]
        turned = [focal[part].T for part in range(2)]
        for part in range(2):
            low, high = turned[part][:, :HALF], turned[part][:, HALF:]
            keep_ref[part, i] = jnp.where(group == 0, low, high)
            send_ref[part, i] = jnp.where(group == 0, high, low)
        real += jnp.dot(turned[0], focal[0], preferred_element_type=jnp.float32)
        real += jnp.dot(turned[1], focal[1], preferred_element_type=jnp.float32)
        cross += jnp.dot(turned[0], focal[1], preferred_element_type=jnp.float32)
    imag = cross - cross.T
    row = lax.broadcasted_iota(jnp.int32, (STACK, STACK), 0)
    column = lax.broadcasted_iota(jnp.int32, (STACK, STACK), 1)
    packed = jnp.where(row <= column, real, imag)
    for q in range(4):
        top, left = (q // 2) * 128, (q % 2) * 128
        gram_ref[pl.ds(q, 128, stride=4), :] = packed[top : top + 128, left : left + 128]


def total_kernel(parts_ref, out_ref):
    total = jnp.sum(parts_ref[...].reshape(DEVICES // 2, 8, 128), axis=0)
    total = total[:4] + total[4:]
    twice = jnp.concatenate([total, total], axis=0)
    out_ref[...] = jnp.broadcast_to(twice[None], (DEVICES // 2, 8, 128)).reshape(4 * DEVICES, 128)


def modes_kernel(group_ref, gram_ref, start_ref, keep_ref, other_ref, out_ref, power_ref, wide_ref):
    highest = lax.Precision.HIGHEST
    quads = [gram_ref[pl.ds(q, 128, stride=4), :] for q in range(4)]
    packed = jnp.concatenate(
        [jnp.concatenate(quads[:2], axis=1), jnp.concatenate(quads[2:], axis=1)], axis=0
    )
    turned = packed.T
    row = lax.broadcasted_iota(jnp.int32, (STACK, STACK), 0)
    column = lax.broadcasted_iota(jnp.int32, (STACK, STACK), 1)
    gram_re = jnp.where(row <= column, packed, turned)
    gram_im = jnp.where(row > column, packed, jnp.where(row == column, 0.0, -turned))

    def product(a, b):
        return jnp.dot(a, b, precision=highest, preferred_element_type=jnp.float32)

    def apply(re, im):
        return (
            product(gram_re, re) - product(gram_im, im),
            product(gram_re, im) + product(gram_im, re),
        )

    basis_re, basis_im = start_ref[0], start_ref[1]
    for _ in range(STEPS):
        image_re, image_im = apply(basis_re, basis_im)
        norm = jnp.sqrt(
            jnp.sum(image_re * image_re + image_im * image_im, axis=0, keepdims=True) + 1e-06
        )
        basis_re = image_re / norm
        basis_im = image_im / norm
    rounded_re = basis_re.astype(jnp.bfloat16)
    rounded_im = basis_im.astype(jnp.bfloat16)
    wide_re = rounded_re.astype(jnp.float32)
    wide_im = rounded_im.astype(jnp.float32)
    image_re, image_im = apply(wide_re, wide_im)
    energy = jnp.sum(wide_re * image_re + wide_im * image_im, axis=0, keepdims=True)
    trace = jnp.sum(jnp.where(row == column, packed, 0.0))
    power_ref[...] = energy * STACK / trace
    inverse = lax.rsqrt(energy / (NROW * NCOL) + 1e-06)
    scale = jnp.broadcast_to(inverse, (RANK, RANK)).T
    left_re = wide_re.T.astype(jnp.bfloat16)
    left_im = wide_im.T.astype(jnp.bfloat16)
    group = group_ref[0]

    def multiply(a, b):
        return jnp.dot(a, b, preferred_element_type=jnp.float32)

    for part in range(2):
        for source, ref in ((0, keep_ref), (1, other_ref)):
            first = jnp.where(group == source, 0, COLS)
            for i in range(COLS):
                focal_re, focal_im = ref[0, i], ref[1, i]
                if part == 0:
                    mode = multiply(left_re, focal_re) - multiply(left_im, focal_im)
                else:
                    mode = multiply(left_re, focal_im) + multiply(left_im, focal_re)
                for lane in range(HALF // 128):
                    rows = pl.ds(lane * WIDE + first + i, RANK, stride=GROUPS * COLS)
                    wide_ref[rows, :] = mode[:, lane * 128 : (lane + 1) * 128] * scale
        for lane in range(HALF // 128):
            out_ref[part, :, :, lane * 128 : (lane + 1) * 128] = (
                wide_ref[lane * WIDE : (lane + 1) * WIDE, :]
                .reshape(RANK, GROUPS * COLS, 128)
                .astype(jnp.bfloat16)
            )


VMEM = pl.BlockSpec(memory_space=pltpu.VMEM)
SMEM = pl.BlockSpec(memory_space=pltpu.SMEM)


def params(mib):
    return pltpu.CompilerParams(vmem_limit_bytes=mib * 1024 * 1024)


def local(fields, lens_phase, occupancy, focus_scale, assignment, start_basis):
    group = lax.axis_index("grp").astype(jnp.int32).reshape(1)
    cos_cols, sin_cols = (jnp.asarray(table) for table in column_tables())
    across = pl.pallas_call(
        spectra_kernel,
        out_shape=jax.ShapeDtypeStruct((DEVICES, COLS, 2 * ROWS, SLOTS), jnp.bfloat16),
        in_specs=[SMEM] * 4 + [VMEM] * 4,
        out_specs=VMEM,
        scratch_shapes=[
            pltpu.VMEM((NCOL // 128 * ROWS * SLOTS, 128), jnp.float32),
            pltpu.VMEM((NCOL // 128 * ROWS * SLOTS, 128), jnp.float32),
            pltpu.VMEM((COLS * BLOCK, SLOTS), jnp.float32),
        ],
        compiler_params=params(20),
        name="spectra",
    )(group, assignment, occupancy, focus_scale, fields[0], lens_phase, cos_cols, sin_cols)
    pieces = lax.all_to_all(across, AXES, 0, 0, tiled=True)
    focal_shape = jax.ShapeDtypeStruct((2, COLS, STACK, HALF), jnp.bfloat16)
    keep, send, gram = pl.pallas_call(
        focal_kernel,
        out_shape=(
            focal_shape,
            focal_shape,
            jax.ShapeDtypeStruct((4 * DEVICES, 128), jnp.float32),
        ),
        in_specs=[SMEM] + [VMEM] * 2,
        out_specs=(VMEM,) * 3,
        compiler_params=params(20),
        name="focal",
    )(group, pieces, jnp.asarray(row_tables()))
    other = lax.ppermute(send, "grp", [(0, 1), (1, 0)])
    parts = lax.all_to_all(gram.reshape(DEVICES, 4, 128), AXES, 0, 0, tiled=True)
    total = pl.pallas_call(
        total_kernel,
        out_shape=jax.ShapeDtypeStruct((4 * DEVICES, 128), jnp.float32),
        in_specs=[VMEM],
        out_specs=VMEM,
        compiler_params=params(4),
        name="total",
    )(parts.reshape(4 * DEVICES, 128))
    whole = lax.all_to_all(total.reshape(DEVICES, 4, 128), AXES, 0, 0, tiled=True)
    coherent_modes, power = pl.pallas_call(
        modes_kernel,
        out_shape=(
            jax.ShapeDtypeStruct((2, RANK, GROUPS * COLS, HALF), jnp.bfloat16),
            jax.ShapeDtypeStruct((1, RANK), jnp.float32),
        ),
        in_specs=[SMEM] + [VMEM] * 4,
        out_specs=(VMEM,) * 2,
        scratch_shapes=[pltpu.VMEM((HALF // 128 * WIDE, 128), jnp.float32)],
        compiler_params=params(20),
        name="modes",
    )(group, whole.reshape(4 * DEVICES, 128), start_basis, keep, other)
    return coherent_modes, power.reshape(RANK)


def solution(mesh):
    in_specs = (P("grp", None, None, "pix", None), P("pix", None), P(), P(), P(), P())
    out_specs = (P(None, None, "pix", "grp"), P())
    return jax.shard_map(local, mesh=mesh, in_specs=in_specs, out_specs=out_specs, check_vma=False)
```

```python
import math

import jax
import jax.numpy as jnp
import numpy as np
from jax import lax
from jax.experimental import pallas as pl
from jax.experimental.pallas import tpu as pltpu
from jax.sharding import PartitionSpec as P

NROW = 512
NCOL = 512
STEPS = 2
GROUPS = 2
PIX = 64
DEVICES = GROUPS * PIX
SLOTS = 128
STACK = GROUPS * SLOTS
RANK = 128
ROWS = NROW // PIX
COLS = NCOL // DEVICES
HALF = NROW // GROUPS
WIDE = RANK * GROUPS * COLS
EARLY = 3
CHUNKS = 4
CHUNK = SLOTS // CHUNKS
BLOCK = DEVICES * 2 * ROWS
AXES = ("grp", "pix")

LIMIT = 0.5 * 1.5 * 3.140625


def fit(function, terms):
    limit = LIMIT * 1.001
    nodes = np.cos(np.pi * (np.arange(400) + 0.5) / 400)
    square = (nodes + 1.0) * 0.5 * limit * limit
    powers = np.stack([square**k for k in range(terms)], axis=1)
    return [float(c) for c in np.linalg.lstsq(powers, function(np.sqrt(square)), rcond=None)[0]]


SIN_FIT = fit(lambda x: np.sin(x) / x, 6)
COS_FIT = fit(np.cos, 7)


def tables(length):
    index = np.arange(length, dtype=np.int64)
    angle = (index[:, None] * index[None, :] % length).astype(np.float32) * np.float32(
        2.0 * math.pi / length
    )
    factor = np.float32(1.0 / math.sqrt(length))
    cosine = (np.cos(angle) * factor).astype(jnp.bfloat16)
    sine = (np.sin(angle) * factor).astype(jnp.bfloat16)
    return cosine, sine


def column_tables():
    i, g, p = np.meshgrid(np.arange(COLS), np.arange(GROUPS), np.arange(PIX), indexing="ij")
    order = (p * (GROUPS * COLS) + g * COLS + i).reshape(-1)
    cosine, sine = tables(NCOL)
    return cosine[order], sine[order]


def row_tables():
    cosine, sine = tables(NROW)
    cosine = cosine.reshape(NROW, PIX, ROWS)
    sine = sine.reshape(NROW, PIX, ROWS)
    real = np.stack([cosine, sine], axis=2).reshape(NROW, 2 * NROW)
    imag = np.stack([-sine, cosine], axis=2).reshape(NROW, 2 * NROW)
    return np.concatenate([real, imag], axis=0)


def polynomial(square, coefficients):
    total = square * coefficients[-1] + coefficients[-2]
    for coefficient in coefficients[-3::-1]:
        total = total * square + coefficient
    return total


def spectra_kernel(
    group_ref, assign_hbm, occ_hbm, chrom_hbm, fields_hbm, lens_hbm, cos_hbm, sin_hbm, out_hbm,
    assign_ref, occ_ref, chrom_ref, fields_ref, lens_ref, cos_ref, sin_ref,
    real_ref, imag_ref, wide_ref, out_ref, small_sem, field_sem, table_sem, out_sem,
):
    def chunk(part, c):
        slots = pl.ds(c * CHUNK, CHUNK)
        return pltpu.make_async_copy(
            fields_hbm.at[part, slots], fields_ref.at[part, slots], field_sem.at[part, c]
        )

    small = [
        pltpu.make_async_copy(source, target, small_sem.at[k])
        for k, (source, target) in enumerate(
            (
                (assign_hbm, assign_ref),
                (occ_hbm, occ_ref),
                (chrom_hbm, chrom_ref),
                (lens_hbm, lens_ref),
            )
        )
    ]
    large = [
        pltpu.make_async_copy(cos_hbm, cos_ref, table_sem.at[0]),
        pltpu.make_async_copy(sin_hbm, sin_ref, table_sem.at[1]),
    ]
    for copy in small:
        copy.start()
    for c in range(CHUNKS):
        for part in range(2):
            chunk(part, c).start()
    for copy in large:
        copy.start()
    for copy in small:
        copy.wait()
    base = group_ref[0] * SLOTS

    def phase(m, carry):
        electron = assign_ref[base + m]
        amplitude = jnp.sqrt(jnp.full((ROWS, 128), occ_ref[electron], jnp.float32))
        twice = amplitude + amplitude
        chromatic = chrom_ref[electron] * 0.5
        for lane in range(NCOL // 128):
            cut = pl.ds(lane * 128, 128)
            half = lens_ref[:, cut] * chromatic
            square = half * half
            sine_half = half * polynomial(square, SIN_FIT)
            scaled = sine_half * twice
            sine = scaled * polynomial(square, COS_FIT)
            cosine = amplitude - scaled * sine_half
            field_re = fields_ref[0, m, :, cut].astype(jnp.float32)
            field_im = fields_ref[1, m, :, cut].astype(jnp.float32)
            rows = pl.ds(pl.multiple_of(lane * ROWS * SLOTS + m * ROWS, ROWS), ROWS)
            real_ref[rows, :] = field_re * cosine - field_im * sine
            imag_ref[rows, :] = field_re * sine + field_im * cosine
        return carry

    for c in range(CHUNKS):
        for part in range(2):
            chunk(part, c).wait()
        lax.fori_loop(c * CHUNK, (c + 1) * CHUNK, phase, 0, unroll=4)
    for copy in large:
        copy.wait()
    contract = (((1,), (1,)), ((), ()))

    def product(table, wave):
        return lax.dot_general(table, wave, contract, preferred_element_type=jnp.float32)

    def wave(ref, j):
        return jnp.concatenate(
            [
                jnp.concatenate(
                    [
                        ref[pl.ds(lane * ROWS * SLOTS + j + q, SLOTS, stride=ROWS), :]
                        for lane in range(NCOL // 128)
                    ],
                    axis=1,
                )
                for q in range(2)
            ],
            axis=0,
        ).astype(jnp.bfloat16)

    cosine = cos_ref[...]
    sine = sin_ref[...]
    for j in range(0, ROWS, 2):
        wave_re = wave(real_ref, j)
        wave_im = wave(imag_ref, j)
        across_re = product(cosine, wave_re) + product(sine, wave_im)
        across_im = product(cosine, wave_im) - product(sine, wave_re)
        for part, across in ((0, across_re), (1, across_im)):
            for q in range(2):
                for i in range(COLS):
                    at = i * BLOCK + part * ROWS + j + q
                    wide_ref[pl.ds(at, DEVICES, stride=2 * ROWS), :] = across[
                        i * DEVICES : (i + 1) * DEVICES, q * SLOTS : (q + 1) * SLOTS
                    ]
    stores = []
    for i in range(COLS):
        out_ref[i] = (
            wide_ref[i * BLOCK : (i + 1) * BLOCK, :]
            .astype(jnp.bfloat16)
            .reshape(DEVICES, 2 * ROWS, SLOTS)
        )
        stores.append(pltpu.make_async_copy(out_ref.at[i], out_hbm.at[:, i], out_sem.at[i]))
        stores[-1].start()
    for copy in stores:
        copy.wait()


def focal_kernel(group_ref, pieces_ref, table_ref, keep_ref, early_ref, late_ref, gram_ref):
    group = group_ref[0]
    real = jnp.zeros((STACK, STACK), jnp.float32)
    cross = jnp.zeros((STACK, STACK), jnp.float32)
    for i in range(COLS):
        wave = jnp.concatenate(
            [
                pieces_ref[g * PIX : (g + 1) * PIX, i].reshape(2 * NROW, SLOTS)
                for g in range(GROUPS)
            ],
            axis=1,
        )
        focal = [
            jnp.dot(
                table_ref[part * NROW : (part + 1) * NROW, :],
                wave,
                preferred_element_type=jnp.float32,
            ).astype(jnp.bfloat16)
            for part in range(2)
        ]
        turned = [focal[part].T for part in range(2)]
        for part in range(2):
            low, high = turned[part][:, :HALF], turned[part][:, HALF:]
            keep_ref[part, i] = jnp.where(group == 0, low, high)
            sent = jnp.where(group == 0, high, low)
            if i < EARLY:
                early_ref[part, i] = sent
            else:
                late_ref[part, i - EARLY] = sent
        real += jnp.dot(turned[0], focal[0], preferred_element_type=jnp.float32)
        real += jnp.dot(turned[1], focal[1], preferred_element_type=jnp.float32)
        cross += jnp.dot(turned[0], focal[1], preferred_element_type=jnp.float32)
    imag = cross - cross.T
    row = lax.broadcasted_iota(jnp.int32, (STACK, STACK), 0)
    column = lax.broadcasted_iota(jnp.int32, (STACK, STACK), 1)
    packed = jnp.where(row <= column, real, imag)
    for q in range(4):
        top, left = (q // 2) * 128, (q % 2) * 128
        gram_ref[pl.ds(q, 128, stride=4), :] = packed[top : top + 128, left : left + 128]


def total_kernel(parts_ref, out_ref):
    total = jnp.sum(parts_ref[...].reshape(DEVICES // 2, 8, 128), axis=0)
    total = total[:4] + total[4:]
    twice = jnp.concatenate([total, total], axis=0)
    out_ref[...] = jnp.broadcast_to(twice[None], (DEVICES // 2, 8, 128)).reshape(4 * DEVICES, 128)


def modes_kernel(group_ref, gram_ref, start_ref, keep_ref, early_ref, late_ref, out_ref, power_ref, wide_ref):
    highest = lax.Precision.HIGHEST
    quads = [gram_ref[pl.ds(q, 128, stride=4), :] for q in range(4)]
    packed = jnp.concatenate(
        [jnp.concatenate(quads[:2], axis=1), jnp.concatenate(quads[2:], axis=1)], axis=0
    )
    turned = packed.T
    row = lax.broadcasted_iota(jnp.int32, (STACK, STACK), 0)
    column = lax.broadcasted_iota(jnp.int32, (STACK, STACK), 1)
    gram_re = jnp.where(row <= column, packed, turned)
    gram_im = jnp.where(row > column, packed, jnp.where(row == column, 0.0, -turned))

    def product(a, b):
        return jnp.dot(a, b, precision=highest, preferred_element_type=jnp.float32)

    def apply(re, im):
        return (
            product(gram_re, re) - product(gram_im, im),
            product(gram_re, im) + product(gram_im, re),
        )

    basis_re, basis_im = start_ref[0], start_ref[1]
    for _ in range(STEPS):
        image_re, image_im = apply(basis_re, basis_im)
        norm = jnp.sqrt(
            jnp.sum(image_re * image_re + image_im * image_im, axis=0, keepdims=True) + 1e-06
        )
        basis_re = image_re / norm
        basis_im = image_im / norm
    rounded_re = basis_re.astype(jnp.bfloat16)
    rounded_im = basis_im.astype(jnp.bfloat16)
    wide_re = rounded_re.astype(jnp.float32)
    wide_im = rounded_im.astype(jnp.float32)
    image_re, image_im = apply(wide_re, wide_im)
    energy = jnp.sum(wide_re * image_re + wide_im * image_im, axis=0, keepdims=True)
    trace = jnp.sum(jnp.where(row == column, packed, 0.0))
    power_ref[...] = energy * STACK / trace
    inverse = lax.rsqrt(energy / (NROW * NCOL) + 1e-06)
    scale = jnp.broadcast_to(inverse, (RANK, RANK)).T
    left_re = wide_re.T.astype(jnp.bfloat16)
    left_im = wide_im.T.astype(jnp.bfloat16)
    group = group_ref[0]

    def multiply(a, b):
        return jnp.dot(a, b, preferred_element_type=jnp.float32)

    for part in range(2):
        for source in range(2):
            first = jnp.where(group == source, 0, COLS)
            for i in range(COLS):
                ref, at = keep_ref, i
                if source == 1:
                    ref, at = (early_ref, i) if i < EARLY else (late_ref, i - EARLY)
                focal_re, focal_im = ref[0, at], ref[1, at]
                if part == 0:
                    mode = multiply(left_re, focal_re) - multiply(left_im, focal_im)
                else:
                    mode = multiply(left_re, focal_im) + multiply(left_im, focal_re)
                for lane in range(HALF // 128):
                    rows = pl.ds(lane * WIDE + first + i, RANK, stride=GROUPS * COLS)
                    wide_ref[rows, :] = mode[:, lane * 128 : (lane + 1) * 128] * scale
        for lane in range(HALF // 128):
            out_ref[part, :, :, lane * 128 : (lane + 1) * 128] = (
                wide_ref[lane * WIDE : (lane + 1) * WIDE, :]
                .reshape(RANK, GROUPS * COLS, 128)
                .astype(jnp.bfloat16)
            )


VMEM = pl.BlockSpec(memory_space=pltpu.VMEM)
HBM = pl.BlockSpec(memory_space=pltpu.HBM)
SMEM = pl.BlockSpec(memory_space=pltpu.SMEM)


def params(mib):
    return pltpu.CompilerParams(vmem_limit_bytes=mib * 1024 * 1024)


def local(fields, lens_phase, occupancy, focus_scale, assignment, start_basis):
    group = lax.axis_index("grp").astype(jnp.int32).reshape(1)
    cos_cols, sin_cols = (jnp.asarray(table) for table in column_tables())
    across = pl.pallas_call(
        spectra_kernel,
        out_shape=jax.ShapeDtypeStruct((DEVICES, COLS, 2 * ROWS, SLOTS), jnp.bfloat16),
        in_specs=[SMEM] + [HBM] * 7,
        out_specs=HBM,
        scratch_shapes=[
            pltpu.SMEM((STACK,), jnp.int32),
            pltpu.SMEM((STACK,), jnp.float32),
            pltpu.SMEM((STACK,), jnp.float32),
            pltpu.VMEM((2, SLOTS, ROWS, NCOL), jnp.bfloat16),
            pltpu.VMEM((ROWS, NCOL), jnp.float32),
            pltpu.VMEM((NCOL, NCOL), jnp.bfloat16),
            pltpu.VMEM((NCOL, NCOL), jnp.bfloat16),
            pltpu.VMEM((NCOL // 128 * ROWS * SLOTS, 128), jnp.float32),
            pltpu.VMEM((NCOL // 128 * ROWS * SLOTS, 128), jnp.float32),
            pltpu.VMEM((COLS * BLOCK, SLOTS), jnp.float32),
            pltpu.VMEM((COLS, DEVICES, 2 * ROWS, SLOTS), jnp.bfloat16),
            pltpu.SemaphoreType.DMA((4,)),
            pltpu.SemaphoreType.DMA((2, CHUNKS)),
            pltpu.SemaphoreType.DMA((2,)),
            pltpu.SemaphoreType.DMA((COLS,)),
        ],
        compiler_params=params(54),
        name="spectra",
    )(group, assignment, occupancy, focus_scale, fields[0], lens_phase, cos_cols, sin_cols)
    pieces = lax.all_to_all(across, AXES, 0, 0, tiled=True)

    def focal_shape(count):
        return jax.ShapeDtypeStruct((2, count, STACK, HALF), jnp.bfloat16)

    keep, early, late, gram = pl.pallas_call(
        focal_kernel,
        out_shape=(
            focal_shape(COLS),
            focal_shape(EARLY),
            focal_shape(COLS - EARLY),
            jax.ShapeDtypeStruct((4 * DEVICES, 128), jnp.float32),
        ),
        in_specs=[SMEM] + [VMEM] * 2,
        out_specs=(VMEM,) * 4,
        compiler_params=params(20),
        name="focal",
    )(group, pieces, jnp.asarray(row_tables()))
    early = lax.ppermute(early, "grp", [(0, 1), (1, 0)])
    late = lax.ppermute(late, "grp", [(0, 1), (1, 0)])
    parts = lax.all_to_all(gram.reshape(DEVICES, 4, 128), AXES, 0, 0, tiled=True)
    total = pl.pallas_call(
        total_kernel,
        out_shape=jax.ShapeDtypeStruct((4 * DEVICES, 128), jnp.float32),
        in_specs=[VMEM],
        out_specs=VMEM,
        compiler_params=params(4),
        name="total",
    )(parts.reshape(4 * DEVICES, 128))
    whole = lax.all_to_all(total.reshape(DEVICES, 4, 128), AXES, 0, 0, tiled=True)
    coherent_modes, power = pl.pallas_call(
        modes_kernel,
        out_shape=(
            jax.ShapeDtypeStruct((2, RANK, GROUPS * COLS, HALF), jnp.bfloat16),
            jax.ShapeDtypeStruct((1, RANK), jnp.float32),
        ),
        in_specs=[SMEM] + [VMEM] * 5,
        out_specs=(VMEM,) * 2,
        scratch_shapes=[pltpu.VMEM((HALF // 128 * WIDE, 128), jnp.float32)],
        compiler_params=params(20),
        name="modes",
    )(group, whole.reshape(4 * DEVICES, 128), start_basis, keep, early, late)
    return coherent_modes, power.reshape(RANK)


def solution(mesh):
    in_specs = (P("grp", None, None, "pix", None), P("pix", None), P(), P(), P(), P())
    out_specs = (P(None, None, "pix", "grp"), P())

    return jax.shard_map(local, mesh=mesh, in_specs=in_specs, out_specs=out_specs, check_vma=False)
```

```python
import math

import jax
import jax.numpy as jnp
import numpy as np
from jax import lax
from jax.experimental import pallas as pl
from jax.experimental.pallas import tpu as pltpu
from jax.sharding import PartitionSpec as P

NROW = 512
NCOL = 512
STEPS = 2
GROUPS = 2
PIX = 64
DEVICES = GROUPS * PIX
SLOTS = 128
STACK = GROUPS * SLOTS
RANK = 128
ROWS = NROW // PIX
COLS = NCOL // DEVICES
HALF = NROW // GROUPS
WIDE = RANK * GROUPS * COLS
EARLY = 2
CHUNKS = 4
CHUNK = SLOTS // CHUNKS
BLOCK = DEVICES * 2 * ROWS
AXES = ("grp", "pix")

LIMIT = 0.5 * 1.5 * 3.140625


def fit(function, terms):
    limit = LIMIT * 1.001
    nodes = np.cos(np.pi * (np.arange(400) + 0.5) / 400)
    square = (nodes + 1.0) * 0.5 * limit * limit
    powers = np.stack([square**k for k in range(terms)], axis=1)
    return [float(c) for c in np.linalg.lstsq(powers, function(np.sqrt(square)), rcond=None)[0]]


SIN_FIT = fit(lambda x: np.sin(x) / x, 6)
COS_FIT = fit(np.cos, 7)


def tables(length):
    index = np.arange(length, dtype=np.int64)
    angle = (index[:, None] * index[None, :] % length).astype(np.float32) * np.float32(
        2.0 * math.pi / length
    )
    factor = np.float32(1.0 / math.sqrt(length))
    cosine = (np.cos(angle) * factor).astype(jnp.bfloat16)
    sine = (np.sin(angle) * factor).astype(jnp.bfloat16)
    return cosine, sine


def column_tables():
    i, g, p = np.meshgrid(np.arange(COLS), np.arange(GROUPS), np.arange(PIX), indexing="ij")
    order = (p * (GROUPS * COLS) + g * COLS + i).reshape(-1)
    cosine, sine = tables(NCOL)
    return cosine[order], sine[order]


def row_tables():
    cosine, sine = tables(NROW)
    cosine = cosine.reshape(NROW, PIX, ROWS)
    sine = sine.reshape(NROW, PIX, ROWS)
    real = np.stack([cosine, sine], axis=2).reshape(NROW, 2 * NROW)
    imag = np.stack([-sine, cosine], axis=2).reshape(NROW, 2 * NROW)
    return np.concatenate([real, imag], axis=0)


def polynomial(square, coefficients):
    total = square * coefficients[-1] + coefficients[-2]
    for coefficient in coefficients[-3::-1]:
        total = total * square + coefficient
    return total


def spectra_kernel(
    group_ref, assign_hbm, occ_hbm, chrom_hbm, fields_hbm, lens_hbm, cos_hbm, sin_hbm, out_hbm,
    assign_ref, occ_ref, chrom_ref, fields_ref, lens_ref, cos_ref, sin_ref,
    real_ref, imag_ref, wide_ref, out_ref, small_sem, field_sem, table_sem, out_sem,
):
    def chunk(part, c):
        slots = pl.ds(c * CHUNK, CHUNK)
        return pltpu.make_async_copy(
            fields_hbm.at[part, slots], fields_ref.at[part, slots], field_sem.at[part, c]
        )

    small = [
        pltpu.make_async_copy(source, target, small_sem.at[k])
        for k, (source, target) in enumerate(
            (
                (assign_hbm, assign_ref),
                (occ_hbm, occ_ref),
                (chrom_hbm, chrom_ref),
                (lens_hbm, lens_ref),
            )
        )
    ]
    large = [
        pltpu.make_async_copy(cos_hbm, cos_ref, table_sem.at[0]),
        pltpu.make_async_copy(sin_hbm, sin_ref, table_sem.at[1]),
    ]
    for copy in small:
        copy.start()
    for c in range(CHUNKS):
        for part in range(2):
            chunk(part, c).start()
    for copy in large:
        copy.start()
    for copy in small:
        copy.wait()
    base = group_ref[0] * SLOTS

    def phase(m, carry):
        electron = assign_ref[base + m]
        amplitude = jnp.sqrt(jnp.full((ROWS, 128), occ_ref[electron], jnp.float32))
        twice = amplitude + amplitude
        chromatic = chrom_ref[electron] * 0.5
        for lane in range(NCOL // 128):
            cut = pl.ds(lane * 128, 128)
            half = lens_ref[:, cut] * chromatic
            square = half * half
            sine_half = half * polynomial(square, SIN_FIT)
            scaled = sine_half * twice
            sine = scaled * polynomial(square, COS_FIT)
            cosine = amplitude - scaled * sine_half
            field_re = fields_ref[0, m, :, cut].astype(jnp.float32)
            field_im = fields_ref[1, m, :, cut].astype(jnp.float32)
            rows = pl.ds(pl.multiple_of(lane * ROWS * SLOTS + m * ROWS, ROWS), ROWS)
            real_ref[rows, :] = field_re * cosine - field_im * sine
            imag_ref[rows, :] = field_re * sine + field_im * cosine
        return carry

    for c in range(CHUNKS):
        for part in range(2):
            chunk(part, c).wait()
        lax.fori_loop(c * CHUNK, (c + 1) * CHUNK, phase, 0, unroll=4)
    for copy in large:
        copy.wait()
    contract = (((1,), (1,)), ((), ()))

    def product(table, wave):
        return lax.dot_general(table, wave, contract, preferred_element_type=jnp.float32)

    def wave(ref, j):
        return jnp.concatenate(
            [
                jnp.concatenate(
                    [
                        ref[pl.ds(lane * ROWS * SLOTS + j + q, SLOTS, stride=ROWS), :]
                        for lane in range(NCOL // 128)
                    ],
                    axis=1,
                )
                for q in range(2)
            ],
            axis=0,
        ).astype(jnp.bfloat16)

    cosine = cos_ref[...]
    sine = sin_ref[...]
    for j in range(0, ROWS, 2):
        wave_re = wave(real_ref, j)
        wave_im = wave(imag_ref, j)
        across_re = product(cosine, wave_re) + product(sine, wave_im)
        across_im = product(cosine, wave_im) - product(sine, wave_re)
        for part, across in ((0, across_re), (1, across_im)):
            for q in range(2):
                for i in range(COLS):
                    at = i * BLOCK + part * ROWS + j + q
                    wide_ref[pl.ds(at, DEVICES, stride=2 * ROWS), :] = across[
                        i * DEVICES : (i + 1) * DEVICES, q * SLOTS : (q + 1) * SLOTS
                    ]
    stores = []
    for i in range(COLS):
        out_ref[i] = (
            wide_ref[i * BLOCK : (i + 1) * BLOCK, :]
            .astype(jnp.bfloat16)
            .reshape(DEVICES, 2 * ROWS, SLOTS)
        )
        stores.append(pltpu.make_async_copy(out_ref.at[i], out_hbm.at[:, i], out_sem.at[i]))
        stores[-1].start()
    for copy in stores:
        copy.wait()


def focal_kernel(group_ref, pieces_ref, table_ref, keep_ref, early_ref, late_ref, gram_ref):
    group = group_ref[0]
    real = jnp.zeros((STACK, STACK), jnp.float32)
    cross = jnp.zeros((STACK, STACK), jnp.float32)
    for i in range(COLS):
        wave = jnp.concatenate(
            [
                pieces_ref[g * PIX : (g + 1) * PIX, i].reshape(2 * NROW, SLOTS)
                for g in range(GROUPS)
            ],
            axis=1,
        )
        focal = [
            jnp.dot(
                table_ref[part * NROW : (part + 1) * NROW, :],
                wave,
                preferred_element_type=jnp.float32,
            ).astype(jnp.bfloat16)
            for part in range(2)
        ]
        turned = [focal[part].T for part in range(2)]
        for part in range(2):
            low, high = turned[part][:, :HALF], turned[part][:, HALF:]
            keep_ref[part, i] = jnp.where(group == 0, low, high)
            sent = jnp.where(group == 0, high, low)
            if i < EARLY:
                early_ref[part, i] = sent
            else:
                late_ref[part, i - EARLY] = sent
        real += jnp.dot(turned[0], focal[0], preferred_element_type=jnp.float32)
        real += jnp.dot(turned[1], focal[1], preferred_element_type=jnp.float32)
        cross += jnp.dot(turned[0], focal[1], preferred_element_type=jnp.float32)
    imag = cross - cross.T
    row = lax.broadcasted_iota(jnp.int32, (STACK, STACK), 0)
    column = lax.broadcasted_iota(jnp.int32, (STACK, STACK), 1)
    packed = jnp.where(row <= column, real, imag)
    for q in range(4):
        top, left = (q // 2) * 128, (q % 2) * 128
        gram_ref[pl.ds(q, 128, stride=4), :] = packed[top : top + 128, left : left + 128]


def total_kernel(parts_ref, out_ref):
    total = jnp.sum(parts_ref[...].reshape(DEVICES // 2, 8, 128), axis=0)
    total = total[:4] + total[4:]
    twice = jnp.concatenate([total, total], axis=0)
    out_ref[...] = jnp.broadcast_to(twice[None], (DEVICES // 2, 8, 128)).reshape(4 * DEVICES, 128)


def power_kernel(gram_ref, start_ref, left_ref, scale_ref, power_ref):
    quads = [gram_ref[pl.ds(q, 128, stride=4), :] for q in range(4)]
    packed = jnp.concatenate(
        [jnp.concatenate(quads[:2], axis=1), jnp.concatenate(quads[2:], axis=1)], axis=0
    )
    turned = packed.T
    row = lax.broadcasted_iota(jnp.int32, (STACK, STACK), 0)
    column = lax.broadcasted_iota(jnp.int32, (STACK, STACK), 1)
    gram_re = jnp.where(row <= column, packed, turned)
    gram_im = jnp.where(row > column, packed, jnp.where(row == column, 0.0, -turned))
    gram = jnp.concatenate([gram_re, gram_im], axis=0)

    def apply(re, im):
        both = jnp.dot(
            gram,
            jnp.concatenate([re, im], axis=1),
            precision=lax.Precision.HIGHEST,
            preferred_element_type=jnp.float32,
        )
        return (
            both[:STACK, :RANK] - both[STACK:, RANK:],
            both[:STACK, RANK:] + both[STACK:, :RANK],
        )

    basis_re, basis_im = start_ref[0], start_ref[1]
    for _ in range(STEPS):
        image_re, image_im = apply(basis_re, basis_im)
        norm = jnp.sqrt(
            jnp.sum(image_re * image_re + image_im * image_im, axis=0, keepdims=True) + 1e-06
        )
        basis_re = image_re / norm
        basis_im = image_im / norm
    rounded_re = basis_re.astype(jnp.bfloat16).astype(jnp.float32)
    rounded_im = basis_im.astype(jnp.bfloat16).astype(jnp.float32)
    image_re, image_im = apply(rounded_re, rounded_im)
    energy = jnp.sum(rounded_re * image_re + rounded_im * image_im, axis=0, keepdims=True)
    trace = jnp.sum(jnp.where(row == column, packed, 0.0))
    power_ref[...] = energy * STACK / trace
    inverse = lax.rsqrt(energy / (NROW * NCOL) + 1e-06)
    scale_ref[...] = jnp.broadcast_to(inverse, (RANK, RANK)).T
    turned_re = rounded_re.T.astype(jnp.bfloat16)
    turned_im = rounded_im.T.astype(jnp.bfloat16)
    left_ref[:RANK, :STACK] = turned_re
    left_ref[:RANK, STACK:] = -turned_im
    left_ref[RANK:, :STACK] = turned_im
    left_ref[RANK:, STACK:] = turned_re


def modes_kernel(
    group_ref, left_ref, scale_ref, keep_ref, early_ref, late_ref, out_hbm,
    wide_ref, out_ref, out_sem,
):
    group = group_ref[0]
    left = left_ref[...]
    scale = scale_ref[...]
    for source in range(2):
        first = jnp.where(group == source, 0, COLS)
        for i in range(COLS):
            ref, at = keep_ref, i
            if source == 1:
                ref, at = (early_ref, i) if i < EARLY else (late_ref, i - EARLY)
            mode = jnp.dot(
                left, ref[:, at].reshape(2 * STACK, HALF), preferred_element_type=jnp.float32
            )
            for part in range(2):
                for lane in range(HALF // 128):
                    rows = pl.ds(
                        (part * 2 + lane) * WIDE + first + i, RANK, stride=GROUPS * COLS
                    )
                    wide_ref[rows, :] = (
                        mode[part * RANK : (part + 1) * RANK, lane * 128 : (lane + 1) * 128] * scale
                    )
    copies = []
    for part in range(2):
        for lane in range(HALF // 128):
            at = (part * 2 + lane) * WIDE
            out_ref[part, :, :, lane * 128 : (lane + 1) * 128] = (
                wide_ref[at : at + WIDE, :].reshape(RANK, GROUPS * COLS, 128).astype(jnp.bfloat16)
            )
        copies.append(pltpu.make_async_copy(out_ref.at[part], out_hbm.at[part], out_sem.at[part]))
        copies[-1].start()
    for copy in copies:
        copy.wait()


VMEM = pl.BlockSpec(memory_space=pltpu.VMEM)
HBM = pl.BlockSpec(memory_space=pltpu.HBM)
SMEM = pl.BlockSpec(memory_space=pltpu.SMEM)


def params(mib):
    return pltpu.CompilerParams(vmem_limit_bytes=mib * 1024 * 1024)


def local(fields, lens_phase, occupancy, focus_scale, assignment, start_basis):
    group = lax.axis_index("grp").astype(jnp.int32).reshape(1)
    cos_cols, sin_cols = (jnp.asarray(table) for table in column_tables())
    across = pl.pallas_call(
        spectra_kernel,
        out_shape=jax.ShapeDtypeStruct((DEVICES, COLS, 2 * ROWS, SLOTS), jnp.bfloat16),
        in_specs=[SMEM] + [HBM] * 7,
        out_specs=HBM,
        scratch_shapes=[
            pltpu.SMEM((STACK,), jnp.int32),
            pltpu.SMEM((STACK,), jnp.float32),
            pltpu.SMEM((STACK,), jnp.float32),
            pltpu.VMEM((2, SLOTS, ROWS, NCOL), jnp.bfloat16),
            pltpu.VMEM((ROWS, NCOL), jnp.float32),
            pltpu.VMEM((NCOL, NCOL), jnp.bfloat16),
            pltpu.VMEM((NCOL, NCOL), jnp.bfloat16),
            pltpu.VMEM((NCOL // 128 * ROWS * SLOTS, 128), jnp.float32),
            pltpu.VMEM((NCOL // 128 * ROWS * SLOTS, 128), jnp.float32),
            pltpu.VMEM((COLS * BLOCK, SLOTS), jnp.float32),
            pltpu.VMEM((COLS, DEVICES, 2 * ROWS, SLOTS), jnp.bfloat16),
            pltpu.SemaphoreType.DMA((4,)),
            pltpu.SemaphoreType.DMA((2, CHUNKS)),
            pltpu.SemaphoreType.DMA((2,)),
            pltpu.SemaphoreType.DMA((COLS,)),
        ],
        compiler_params=params(54),
        name="spectra",
    )(group, assignment, occupancy, focus_scale, fields[0], lens_phase, cos_cols, sin_cols)
    pieces = lax.all_to_all(across, AXES, 0, 0, tiled=True)

    def focal_shape(count):
        return jax.ShapeDtypeStruct((2, count, STACK, HALF), jnp.bfloat16)

    keep, early, late, gram = pl.pallas_call(
        focal_kernel,
        out_shape=(
            focal_shape(COLS),
            focal_shape(EARLY),
            focal_shape(COLS - EARLY),
            jax.ShapeDtypeStruct((4 * DEVICES, 128), jnp.float32),
        ),
        in_specs=[SMEM] + [VMEM] * 2,
        out_specs=(VMEM,) * 4,
        compiler_params=params(20),
        name="focal",
    )(group, pieces, jnp.asarray(row_tables()))
    early = lax.ppermute(early, "grp", [(0, 1), (1, 0)])
    late = lax.ppermute(late, "grp", [(0, 1), (1, 0)])
    parts = lax.all_to_all(gram.reshape(DEVICES, 4, 128), AXES, 0, 0, tiled=True)
    total = pl.pallas_call(
        total_kernel,
        out_shape=jax.ShapeDtypeStruct((4 * DEVICES, 128), jnp.float32),
        in_specs=[VMEM],
        out_specs=VMEM,
        compiler_params=params(4),
        name="total",
    )(parts.reshape(4 * DEVICES, 128))
    whole = lax.all_to_all(total.reshape(DEVICES, 4, 128), AXES, 0, 0, tiled=True)
    left, scale, power = pl.pallas_call(
        power_kernel,
        out_shape=(
            jax.ShapeDtypeStruct((2 * RANK, 2 * STACK), jnp.bfloat16),
            jax.ShapeDtypeStruct((RANK, RANK), jnp.float32),
            jax.ShapeDtypeStruct((1, RANK), jnp.float32),
        ),
        in_specs=[VMEM] * 2,
        out_specs=(VMEM,) * 3,
        compiler_params=params(12),
        name="power",
    )(whole.reshape(4 * DEVICES, 128), start_basis)
    coherent_modes = pl.pallas_call(
        modes_kernel,
        out_shape=jax.ShapeDtypeStruct((2, RANK, GROUPS * COLS, HALF), jnp.bfloat16),
        in_specs=[SMEM] + [VMEM] * 5,
        out_specs=HBM,
        scratch_shapes=[
            pltpu.VMEM((2 * HALF // 128 * WIDE, 128), jnp.float32),
            pltpu.VMEM((2, RANK, GROUPS * COLS, HALF), jnp.bfloat16),
            pltpu.SemaphoreType.DMA((2,)),
        ],
        compiler_params=params(16),
        name="modes",
    )(group, left, scale, keep, early, late)
    return coherent_modes, power.reshape(RANK)


def solution(mesh):
    in_specs = (P("grp", None, None, "pix", None), P("pix", None), P(), P(), P(), P())
    out_specs = (P(None, None, "pix", "grp"), P())

    return jax.shard_map(local, mesh=mesh, in_specs=in_specs, out_specs=out_specs, check_vma=False)
```

```python
import math

import jax
import jax.numpy as jnp
import numpy as np
from jax import lax
from jax.experimental import pallas as pl
from jax.experimental.pallas import tpu as pltpu
from jax.sharding import PartitionSpec as P

NROW = 512
NCOL = 512
STEPS = 2
GROUPS = 2
PIX = 64
DEVICES = GROUPS * PIX
SLOTS = 128
STACK = GROUPS * SLOTS
RANK = 128
ROWS = NROW // PIX
COLS = NCOL // DEVICES
HALF = NROW // GROUPS
WIDE = RANK * GROUPS * COLS
THIRD = 2
CHUNKS = 4
CHUNK = SLOTS // CHUNKS
BLOCK = DEVICES * 2 * ROWS
AXES = ("grp", "pix")

LIMIT = 0.5 * 1.5 * 3.140625


def fit(function, terms):
    limit = LIMIT * 1.001
    nodes = np.cos(np.pi * (np.arange(400) + 0.5) / 400)
    square = (nodes + 1.0) * 0.5 * limit * limit
    powers = np.stack([square**k for k in range(terms)], axis=1)
    return [float(c) for c in np.linalg.lstsq(powers, function(np.sqrt(square)), rcond=None)[0]]


SIN_FIT = fit(lambda x: np.sin(x) / x, 6)
COS_FIT = fit(np.cos, 7)


def tables(length):
    index = np.arange(length, dtype=np.int64)
    angle = (index[:, None] * index[None, :] % length).astype(np.float32) * np.float32(
        2.0 * math.pi / length
    )
    factor = np.float32(1.0 / math.sqrt(length))
    cosine = (np.cos(angle) * factor).astype(jnp.bfloat16)
    sine = (np.sin(angle) * factor).astype(jnp.bfloat16)
    return cosine, sine


def column_tables():
    i, g, p = np.meshgrid(
        np.arange(COLS), np.arange(GROUPS), np.arange(PIX // 2), indexing="ij"
    )
    order = (p * (GROUPS * COLS) + g * COLS + i).reshape(-1)
    pair = np.arange(0, NCOL, 256)[:, None]
    lane = np.arange(64)
    even = np.concatenate([pair + 2 * lane, pair + 128 + 2 * lane], axis=1).reshape(-1)
    odd = np.concatenate([pair + 129 + 2 * lane, pair + 1 + 2 * lane], axis=1).reshape(-1)
    cosine, sine = (table[order] for table in tables(NCOL))
    return np.stack(
        [
            np.block([[cosine[:, k], sine[:, k]], [-sine[:, k], cosine[:, k]]])
            for k in (even, odd)
        ]
    )


def row_tables():
    cosine, sine = (
        table[:HALF].reshape(HALF, PIX, ROWS // 2, 2).transpose(3, 0, 1, 2)
        for table in tables(NROW)
    )
    real = np.stack([cosine, sine], axis=3).reshape(2, HALF, NROW)
    imag = np.stack([-sine, cosine], axis=3).reshape(2, HALF, NROW)
    return np.concatenate([real, imag], axis=1)


def polynomial(square, coefficients):
    total = square * coefficients[-1] + coefficients[-2]
    for coefficient in coefficients[-3::-1]:
        total = total * square + coefficient
    return total


def spectra_kernel(
    group_ref, assign_hbm, occ_hbm, chrom_hbm, fields_hbm, lens_hbm, table_hbm, out_hbm,
    assign_ref, occ_ref, chrom_ref, fields_ref, lens_ref, table_ref,
    real_ref, imag_ref, wide_ref, out_ref, small_sem, field_sem, table_sem, out_sem,
):
    def chunk(part, c):
        slots = pl.ds(c * CHUNK, CHUNK)
        return pltpu.make_async_copy(
            fields_hbm.at[part, slots], fields_ref.at[part, slots], field_sem.at[part, c]
        )

    small = [
        pltpu.make_async_copy(source, target, small_sem.at[k])
        for k, (source, target) in enumerate(
            (
                (assign_hbm, assign_ref),
                (occ_hbm, occ_ref),
                (chrom_hbm, chrom_ref),
                (lens_hbm, lens_ref),
            )
        )
    ]
    large = [
        pltpu.make_async_copy(table_hbm.at[odd], table_ref.at[odd], table_sem.at[odd])
        for odd in range(2)
    ]
    for copy in small:
        copy.start()
    for c in range(CHUNKS):
        for part in range(2):
            chunk(part, c).start()
    for copy in large:
        copy.start()
    for copy in small:
        copy.wait()
    base = group_ref[0] * SLOTS

    def phase(m, carry):
        electron = assign_ref[base + m]
        amplitude = jnp.sqrt(jnp.full((ROWS, 128), occ_ref[electron], jnp.float32))
        twice = amplitude + amplitude
        chromatic = chrom_ref[electron] * 0.5
        for lane in range(NCOL // 128):
            cut = pl.ds(lane * 128, 128)
            half = lens_ref[:, cut] * chromatic
            square = half * half
            sine_half = half * polynomial(square, SIN_FIT)
            scaled = sine_half * twice
            sine = scaled * polynomial(square, COS_FIT)
            cosine = amplitude - scaled * sine_half
            field_re = fields_ref[0, m, :, cut].astype(jnp.float32)
            field_im = fields_ref[1, m, :, cut].astype(jnp.float32)
            rows = pl.ds(pl.multiple_of(lane * ROWS * SLOTS + m * ROWS, ROWS), ROWS)
            real_ref[rows, :] = field_re * cosine - field_im * sine
            imag_ref[rows, :] = field_re * sine + field_im * cosine
        return carry

    for c in range(CHUNKS):
        for part in range(2):
            chunk(part, c).wait()
        lax.fori_loop(c * CHUNK, (c + 1) * CHUNK, phase, 0, unroll=4)
    for copy in large:
        copy.wait()
    lane = lax.broadcasted_iota(jnp.int32, (SLOTS, 128), 1)
    evens_first = 2 * (lane % 64) + lane // 64
    odds_first = 2 * (lane % 64) + 1 - lane // 64

    def parts(ref, j):
        even, odd = [], []
        for tile in range(0, NCOL // 128, 2):
            left, right = (
                ref[pl.ds((tile + k) * ROWS * SLOTS + j, SLOTS, stride=ROWS), :] for k in range(2)
            )
            left = jnp.take_along_axis(left, evens_first, axis=1)
            right = jnp.take_along_axis(right, odds_first, axis=1)
            even.append(jnp.where(lane < 64, left, right))
            odd.append(jnp.where(lane < 64, right, left))
        return even, odd

    contract = (((1,), (1,)), ((), ()))
    for j in range(0, ROWS, 2):
        waves = [[], []]
        for q in range(2):
            real, imag = parts(real_ref, j + q), parts(imag_ref, j + q)
            for odd in range(2):
                waves[odd].append(jnp.concatenate(real[odd] + imag[odd], axis=1))
        even, odd = (
            lax.dot_general(
                table_ref[k],
                jnp.concatenate(waves[k], axis=0).astype(jnp.bfloat16),
                contract,
                preferred_element_type=jnp.float32,
            )
            for k in range(2)
        )
        for half, across in ((0, even + odd), (1, even - odd)):
            for q in range(2):
                for part in range(2):
                    for block in range(COLS * GROUPS):
                        i, g = block // GROUPS, block % GROUPS
                        device = g * PIX + half * (PIX // 2)
                        at = i * BLOCK + device * 2 * ROWS + q * ROWS + part * (ROWS // 2) + j // 2
                        row = part * (NCOL // 2) + block * (PIX // 2)
                        wide_ref[pl.ds(at, PIX // 2, stride=2 * ROWS), :] = across[
                            row : row + PIX // 2, q * SLOTS : (q + 1) * SLOTS
                        ]
    stores = []
    for i in range(COLS):
        out_ref[i] = (
            wide_ref[i * BLOCK : (i + 1) * BLOCK, :]
            .astype(jnp.bfloat16)
            .reshape(DEVICES, 2 * ROWS, SLOTS)
        )
        stores.append(pltpu.make_async_copy(out_ref.at[i], out_hbm.at[:, i], out_sem.at[i]))
        stores[-1].start()
    for copy in stores:
        copy.wait()


def focal_column(pieces_ref, table_ref, i):
    halves = []
    for odd in range(2):
        wave = jnp.concatenate(
            [
                pieces_ref[g * PIX : (g + 1) * PIX, i, odd].reshape(NROW, SLOTS)
                for g in range(GROUPS)
            ],
            axis=1,
        )
        halves.append(jnp.dot(table_ref[odd], wave, preferred_element_type=jnp.float32))
    low = (halves[0] + halves[1]).astype(jnp.bfloat16)
    high = (halves[0] - halves[1]).astype(jnp.bfloat16)
    return [
        jnp.concatenate([half[part * HALF : (part + 1) * HALF] for half in (low, high)], axis=0)
        for part in range(2)
    ]


def add_gram(focal, turned, real, cross):
    real += jnp.dot(turned[0], focal[0], preferred_element_type=jnp.float32)
    real += jnp.dot(turned[1], focal[1], preferred_element_type=jnp.float32)
    cross += jnp.dot(turned[0], focal[1], preferred_element_type=jnp.float32)
    return real, cross


def split(group, turned):
    low, high = turned[:, :HALF], turned[:, HALF:]
    return jnp.where(group == 0, low, high), jnp.where(group == 0, high, low)


def focal_kernel(group_ref, pieces_ref, table_ref, keep_ref, send_ref, real_ref, cross_ref):
    focal = focal_column(pieces_ref, table_ref, 0)
    turned = [focal[part].T for part in range(2)]
    for part in range(2):
        keep_ref[part], send_ref[part] = split(group_ref[0], turned[part])
    zero = jnp.zeros((STACK, STACK), jnp.float32)
    real_ref[...], cross_ref[...] = add_gram(focal, turned, zero, zero)


def more_focal_kernel(
    group_ref, pieces_ref, table_ref, real_ref, cross_ref, keep_ref, second_ref, third_hbm, gram_ref,
    third_ref, third_sem,
):
    real, cross = real_ref[...], cross_ref[...]
    for i in range(1, COLS):
        focal = focal_column(pieces_ref, table_ref, i)
        turned = [focal[part].T for part in range(2)]
        for part in range(2):
            at = (i - 1) * 2 + part
            kept, sent = split(group_ref[0], turned[part])
            keep_ref[at] = kept
            if at < THIRD:
                third_ref[at] = sent
            else:
                second_ref[at - THIRD] = sent
        if i * 2 == THIRD:
            late = pltpu.make_async_copy(third_ref, third_hbm, third_sem)
            late.start()
        real, cross = add_gram(focal, turned, real, cross)
    imag = cross - cross.T
    row = lax.broadcasted_iota(jnp.int32, (STACK, STACK), 0)
    column = lax.broadcasted_iota(jnp.int32, (STACK, STACK), 1)
    packed = jnp.where(row <= column, real, imag)
    for q in range(4):
        top, left = (q // 2) * 128, (q % 2) * 128
        gram_ref[pl.ds(q, 128, stride=4), :] = packed[top : top + 128, left : left + 128]
    late.wait()


def total_kernel(parts_ref, out_ref):
    total = jnp.sum(parts_ref[...].reshape(DEVICES // 2, 8, 128), axis=0)
    total = total[:4] + total[4:]
    twice = jnp.concatenate([total, total], axis=0)
    out_ref[...] = jnp.broadcast_to(twice[None], (DEVICES // 2, 8, 128)).reshape(4 * DEVICES, 128)


def power_kernel(gram_ref, start_ref, left_ref, scale_ref, power_ref):
    quads = [gram_ref[pl.ds(q, 128, stride=4), :] for q in range(4)]
    packed = jnp.concatenate(
        [jnp.concatenate(quads[:2], axis=1), jnp.concatenate(quads[2:], axis=1)], axis=0
    )
    turned = packed.T
    row = lax.broadcasted_iota(jnp.int32, (STACK, STACK), 0)
    column = lax.broadcasted_iota(jnp.int32, (STACK, STACK), 1)
    gram_re = jnp.where(row <= column, packed, turned)
    gram_im = jnp.where(row > column, packed, jnp.where(row == column, 0.0, -turned))
    gram = jnp.concatenate([gram_re, gram_im], axis=0)

    def apply(re, im):
        both = jnp.dot(
            gram,
            jnp.concatenate([re, im], axis=1),
            precision=lax.Precision.HIGHEST,
            preferred_element_type=jnp.float32,
        )
        return (
            both[:STACK, :RANK] - both[STACK:, RANK:],
            both[:STACK, RANK:] + both[STACK:, :RANK],
        )

    basis_re, basis_im = start_ref[0], start_ref[1]
    for _ in range(STEPS):
        image_re, image_im = apply(basis_re, basis_im)
        norm = jnp.sqrt(
            jnp.sum(image_re * image_re + image_im * image_im, axis=0, keepdims=True) + 1e-06
        )
        basis_re = image_re / norm
        basis_im = image_im / norm
    rounded_re = basis_re.astype(jnp.bfloat16).astype(jnp.float32)
    rounded_im = basis_im.astype(jnp.bfloat16).astype(jnp.float32)
    image_re, image_im = apply(rounded_re, rounded_im)
    energy = jnp.sum(rounded_re * image_re + rounded_im * image_im, axis=0, keepdims=True)
    trace = jnp.sum(jnp.where(row == column, packed, 0.0))
    power_ref[...] = energy * STACK / trace
    inverse = lax.rsqrt(energy / (NROW * NCOL) + 1e-06)
    scale_ref[...] = jnp.broadcast_to(inverse, (RANK, RANK)).T
    turned_re = rounded_re.T.astype(jnp.bfloat16)
    turned_im = rounded_im.T.astype(jnp.bfloat16)
    left_ref[:RANK, :STACK] = turned_re
    left_ref[:RANK, STACK:] = -turned_im
    left_ref[RANK:, :STACK] = turned_im
    left_ref[RANK:, STACK:] = turned_re


def modes_kernel(
    group_ref, left_ref, scale_ref, kept_ref, kept_more_ref, first_ref, second_ref, third_ref,
    out_hbm,    wide_ref, out_ref, out_sem,
):
    group = group_ref[0]
    left = left_ref[...]
    scale = scale_ref[...]
    sources = (
        [kept_ref[part] for part in range(2)] + [kept_more_ref[at] for at in range(2 * COLS - 2)],
        [first_ref[part] for part in range(2)]
        + [third_ref[at] for at in range(THIRD)]
        + [second_ref[at] for at in range(2 * COLS - 2 - THIRD)],
    )
    for source in range(2):
        first = jnp.where(group == source, 0, COLS)
        for i in range(COLS):
            focal = jnp.concatenate(sources[source][2 * i : 2 * i + 2], axis=0)
            mode = jnp.dot(left, focal, preferred_element_type=jnp.float32)
            for part in range(2):
                for lane in range(HALF // 128):
                    rows = pl.ds(
                        (part * 2 + lane) * WIDE + first + i, RANK, stride=GROUPS * COLS
                    )
                    wide_ref[rows, :] = (
                        mode[part * RANK : (part + 1) * RANK, lane * 128 : (lane + 1) * 128] * scale
                    )
    copies = []
    for part in range(2):
        for lane in range(HALF // 128):
            at = (part * 2 + lane) * WIDE
            out_ref[part, :, :, lane * 128 : (lane + 1) * 128] = (
                wide_ref[at : at + WIDE, :].reshape(RANK, GROUPS * COLS, 128).astype(jnp.bfloat16)
            )
        copies.append(pltpu.make_async_copy(out_ref.at[part], out_hbm.at[part], out_sem.at[part]))
        copies[-1].start()
    for copy in copies:
        copy.wait()


VMEM = pl.BlockSpec(memory_space=pltpu.VMEM)
HBM = pl.BlockSpec(memory_space=pltpu.HBM)
SMEM = pl.BlockSpec(memory_space=pltpu.SMEM)


def params(mib):
    return pltpu.CompilerParams(vmem_limit_bytes=mib * 1024 * 1024)


def local(fields, lens_phase, occupancy, focus_scale, assignment, start_basis):
    group = lax.axis_index("grp").astype(jnp.int32).reshape(1)
    column_table = jnp.asarray(column_tables())
    across = pl.pallas_call(
        spectra_kernel,
        out_shape=jax.ShapeDtypeStruct((DEVICES, COLS, 2 * ROWS, SLOTS), jnp.bfloat16),
        in_specs=[SMEM] + [HBM] * 6,
        out_specs=HBM,
        scratch_shapes=[
            pltpu.SMEM((STACK,), jnp.int32),
            pltpu.SMEM((STACK,), jnp.float32),
            pltpu.SMEM((STACK,), jnp.float32),
            pltpu.VMEM((2, SLOTS, ROWS, NCOL), jnp.bfloat16),
            pltpu.VMEM((ROWS, NCOL), jnp.float32),
            pltpu.VMEM((2, NCOL, NCOL), jnp.bfloat16),
            pltpu.VMEM((NCOL // 128 * ROWS * SLOTS, 128), jnp.float32),
            pltpu.VMEM((NCOL // 128 * ROWS * SLOTS, 128), jnp.float32),
            pltpu.VMEM((COLS * BLOCK, SLOTS), jnp.float32),
            pltpu.VMEM((COLS, DEVICES, 2 * ROWS, SLOTS), jnp.bfloat16),
            pltpu.SemaphoreType.DMA((4,)),
            pltpu.SemaphoreType.DMA((2, CHUNKS)),
            pltpu.SemaphoreType.DMA((2,)),
            pltpu.SemaphoreType.DMA((COLS,)),
        ],
        compiler_params=params(54),
        name="spectra",
    )(group, assignment, occupancy, focus_scale, fields[0], lens_phase, column_table)
    pieces = lax.all_to_all(across, AXES, 0, 0, tiled=True)
    pieces = pieces.reshape(DEVICES, COLS, 2, ROWS, SLOTS)


    def focal_shape(count):
        return jax.ShapeDtypeStruct((count, STACK, HALF), jnp.bfloat16)

    row_table = jnp.asarray(row_tables())
    square = jax.ShapeDtypeStruct((STACK, STACK), jnp.float32)
    kept, swap_first, real, cross = pl.pallas_call(
        focal_kernel,
        out_shape=(focal_shape(2), focal_shape(2), square, square),
        in_specs=[SMEM] + [VMEM] * 2,
        out_specs=(VMEM,) * 4,
        compiler_params=params(12),
        name="focal",
    )(group, pieces, row_table)
    kept_more, swap_second, swap_third, gram = pl.pallas_call(
        more_focal_kernel,
        out_shape=(
            focal_shape(2 * COLS - 2),
            focal_shape(2 * COLS - 2 - THIRD),
            pltpu.HBM((THIRD, STACK, HALF), jnp.bfloat16),
            jax.ShapeDtypeStruct((4 * DEVICES, 128), jnp.float32),
        ),
        in_specs=[SMEM] + [VMEM] * 4,
        out_specs=(VMEM, VMEM, HBM, VMEM),
        scratch_shapes=[pltpu.VMEM((THIRD, STACK, HALF), jnp.bfloat16), pltpu.SemaphoreType.DMA],
        compiler_params=params(12),
        name="more_focal",
    )(group, pieces, row_table, real, cross)
    swap_first = lax.ppermute(swap_first, "grp", [(0, 1), (1, 0)])
    swap_second = lax.ppermute(swap_second, "grp", [(0, 1), (1, 0)])
    swap_third = lax.ppermute(swap_third, "grp", [(0, 1), (1, 0)])
    parts = lax.all_to_all(gram.reshape(DEVICES, 4, 128), AXES, 0, 0, tiled=True)
    total = pl.pallas_call(
        total_kernel,
        out_shape=jax.ShapeDtypeStruct((4 * DEVICES, 128), jnp.float32),
        in_specs=[VMEM],
        out_specs=VMEM,
        compiler_params=params(4),
        name="total",
    )(parts.reshape(4 * DEVICES, 128))
    whole = lax.all_to_all(total.reshape(DEVICES, 4, 128), AXES, 0, 0, tiled=True)
    left, scale, power = pl.pallas_call(
        power_kernel,
        out_shape=(
            jax.ShapeDtypeStruct((2 * RANK, 2 * STACK), jnp.bfloat16),
            jax.ShapeDtypeStruct((RANK, RANK), jnp.float32),
            jax.ShapeDtypeStruct((1, RANK), jnp.float32),
        ),
        in_specs=[VMEM] * 2,
        out_specs=(VMEM,) * 3,
        compiler_params=params(12),
        name="power",
    )(whole.reshape(4 * DEVICES, 128), start_basis)
    coherent_modes = pl.pallas_call(
        modes_kernel,
        out_shape=jax.ShapeDtypeStruct((2, RANK, GROUPS * COLS, HALF), jnp.bfloat16),
        in_specs=[SMEM] + [VMEM] * 7,
        out_specs=HBM,
        scratch_shapes=[
            pltpu.VMEM((2 * HALF // 128 * WIDE, 128), jnp.float32),
            pltpu.VMEM((2, RANK, GROUPS * COLS, HALF), jnp.bfloat16),
            pltpu.SemaphoreType.DMA((2,)),
        ],
        compiler_params=params(16),
        name="modes",
    )(group, left, scale, kept, kept_more, swap_first, swap_second, swap_third)
    return coherent_modes, power.reshape(RANK)


def solution(mesh):
    in_specs = (P("grp", None, None, "pix", None), P("pix", None), P(), P(), P(), P())
    out_specs = (P(None, None, "pix", "grp"), P())

    return jax.shard_map(local, mesh=mesh, in_specs=in_specs, out_specs=out_specs, check_vma=False)
```

```python
import math

import jax
import jax.numpy as jnp
import numpy as np
from jax import lax
from jax.experimental import pallas as pl
from jax.experimental.pallas import tpu as pltpu
from jax.sharding import PartitionSpec as P

NROW = 512
NCOL = 512
STEPS = 2
GROUPS = 2
PIX = 64
DEVICES = GROUPS * PIX
SLOTS = 128
STACK = GROUPS * SLOTS
RANK = 128
ROWS = NROW // PIX
COLS = NCOL // DEVICES
HALF = NROW // GROUPS
WIDE = RANK * GROUPS * COLS
THIRD = 2
CHUNKS = 4
CHUNK = SLOTS // CHUNKS
PLANE = DEVICES * COLS + 1
AXES = ("grp", "pix")

LIMIT = 0.5 * 1.5 * 3.140625


def fit(function, terms):
    limit = LIMIT * 1.001
    nodes = np.cos(np.pi * (np.arange(400) + 0.5) / 400)
    square = (nodes + 1.0) * 0.5 * limit * limit
    powers = np.stack([square**k for k in range(terms)], axis=1)
    return [float(c) for c in np.linalg.lstsq(powers, function(np.sqrt(square)), rcond=None)[0]]


SIN_FIT = fit(lambda x: np.sin(x) / x, 6)
COS_FIT = fit(np.cos, 7)


def tables(length):
    index = np.arange(length, dtype=np.int64)
    angle = (index[:, None] * index[None, :] % length).astype(np.float32) * np.float32(
        2.0 * math.pi / length
    )
    factor = np.float32(1.0 / math.sqrt(length))
    cosine = (np.cos(angle) * factor).astype(jnp.bfloat16)
    sine = (np.sin(angle) * factor).astype(jnp.bfloat16)
    return cosine, sine


def column_tables():
    i, g, p = np.meshgrid(
        np.arange(COLS), np.arange(GROUPS), np.arange(PIX // 2), indexing="ij"
    )
    order = (p * (GROUPS * COLS) + g * COLS + i).reshape(-1)
    pair = np.arange(0, NCOL, 256)[:, None]
    lane = np.arange(64)
    even = np.concatenate([pair + 2 * lane, pair + 128 + 2 * lane], axis=1).reshape(-1)
    odd = np.concatenate([pair + 129 + 2 * lane, pair + 1 + 2 * lane], axis=1).reshape(-1)
    cosine, sine = (table[order] for table in tables(NCOL))
    return np.stack(
        [
            np.block([[cosine[:, k], sine[:, k]], [-sine[:, k], cosine[:, k]]])
            for k in (even, odd)
        ]
    )


def row_tables():
    cosine, sine = (
        table[:HALF].reshape(HALF, PIX, ROWS // 2, 2).transpose(3, 0, 1, 2)
        for table in tables(NROW)
    )
    real = np.stack([cosine, sine], axis=3).reshape(2, HALF, NROW)
    imag = np.stack([-sine, cosine], axis=3).reshape(2, HALF, NROW)
    return np.concatenate([real, imag], axis=1)


def polynomial(square, coefficients):
    total = square * coefficients[-1] + coefficients[-2]
    for coefficient in coefficients[-3::-1]:
        total = total * square + coefficient
    return total


def spectra_kernel(
    group_ref, assign_hbm, occ_hbm, chrom_hbm, fields_hbm, lens_hbm, table_hbm, out_ref,
    assign_ref, occ_ref, chrom_ref, fields_ref, lens_ref, table_ref,
    real_ref, imag_ref, wide_ref, small_sem, field_sem, table_sem,
):
    def chunk(part, c):
        slots = pl.ds(c * CHUNK, CHUNK)
        return pltpu.make_async_copy(
            fields_hbm.at[part, slots], fields_ref.at[part, slots], field_sem.at[part, c]
        )

    small = [
        pltpu.make_async_copy(source, target, small_sem.at[k])
        for k, (source, target) in enumerate(
            (
                (assign_hbm, assign_ref),
                (occ_hbm, occ_ref),
                (chrom_hbm, chrom_ref),
                (lens_hbm, lens_ref),
            )
        )
    ]
    large = [
        pltpu.make_async_copy(table_hbm.at[odd], table_ref.at[odd], table_sem.at[odd])
        for odd in range(2)
    ]
    for copy in small:
        copy.start()
    for c in range(CHUNKS):
        for part in range(2):
            chunk(part, c).start()
    for copy in large:
        copy.start()
    for copy in small:
        copy.wait()
    base = group_ref[0] * SLOTS

    def phase(m, carry):
        electron = assign_ref[base + m]
        amplitude = jnp.sqrt(jnp.full((ROWS, 128), occ_ref[electron], jnp.float32))
        twice = amplitude + amplitude
        chromatic = chrom_ref[electron] * 0.5
        for lane in range(NCOL // 128):
            cut = pl.ds(lane * 128, 128)
            half = lens_ref[:, cut] * chromatic
            square = half * half
            sine_half = half * polynomial(square, SIN_FIT)
            scaled = sine_half * twice
            sine = scaled * polynomial(square, COS_FIT)
            cosine = amplitude - scaled * sine_half
            field_re = fields_ref[0, m, :, cut].astype(jnp.float32)
            field_im = fields_ref[1, m, :, cut].astype(jnp.float32)
            rows = pl.ds(pl.multiple_of(lane * ROWS * SLOTS + m * ROWS, ROWS), ROWS)
            real_ref[rows, :] = field_re * cosine - field_im * sine
            imag_ref[rows, :] = field_re * sine + field_im * cosine
        return carry

    for c in range(CHUNKS):
        for part in range(2):
            chunk(part, c).wait()
        lax.fori_loop(c * CHUNK, (c + 1) * CHUNK, phase, 0, unroll=16)
    for copy in large:
        copy.wait()
    lane = lax.broadcasted_iota(jnp.int32, (SLOTS, 128), 1)
    evens_first = 2 * (lane % 64) + lane // 64
    odds_first = 2 * (lane % 64) + 1 - lane // 64

    def parts(ref, j):
        even, odd = [], []
        for tile in range(0, NCOL // 128, 2):
            left, right = (
                ref[pl.ds((tile + k) * ROWS * SLOTS + j, SLOTS, stride=ROWS), :] for k in range(2)
            )
            left = jnp.take_along_axis(left, evens_first, axis=1)
            right = jnp.take_along_axis(right, odds_first, axis=1)
            even.append(jnp.where(lane < 64, left, right))
            odd.append(jnp.where(lane < 64, right, left))
        return even, odd

    contract = (((1,), (1,)), ((), ()))
    for j in range(0, ROWS, 2):
        waves = [[], []]
        for q in range(2):
            real, imag = parts(real_ref, j + q), parts(imag_ref, j + q)
            for odd in range(2):
                waves[odd].append(jnp.concatenate(real[odd] + imag[odd], axis=1))
        even, odd = (
            lax.dot_general(
                table_ref[k],
                jnp.concatenate(waves[k], axis=0).astype(jnp.bfloat16),
                contract,
                preferred_element_type=jnp.float32,
            )
            for k in range(2)
        )
        for half, across in ((0, even + odd), (1, even - odd)):
            for q in range(2):
                for part in range(2):
                    for block in range(COLS * GROUPS):
                        i, g = block // GROUPS, block % GROUPS
                        device = g * PIX + half * (PIX // 2)
                        at = q * ROWS + part * (ROWS // 2) + j // 2
                        row = part * (NCOL // 2) + block * (PIX // 2)
                        wide_ref[pl.ds(at * PLANE + i * DEVICES + device, PIX // 2), :] = across[
                            row : row + PIX // 2, q * SLOTS : (q + 1) * SLOTS
                        ]
    for i in range(COLS):

        def gather(d, carry):
            rows = wide_ref[pl.ds(i * DEVICES + d, 2 * ROWS, stride=PLANE), :]
            out_ref[d, i] = rows.astype(jnp.bfloat16)
            return carry

        lax.fori_loop(0, DEVICES, gather, 0, unroll=8)


def focal_column(pieces_ref, table_ref, i):
    halves = []
    for odd in range(2):
        wave = jnp.concatenate(
            [
                pieces_ref[g * PIX : (g + 1) * PIX, i, odd].reshape(NROW, SLOTS)
                for g in range(GROUPS)
            ],
            axis=1,
        )
        halves.append(jnp.dot(table_ref[odd], wave, preferred_element_type=jnp.float32))
    low = (halves[0] + halves[1]).astype(jnp.bfloat16)
    high = (halves[0] - halves[1]).astype(jnp.bfloat16)
    return [
        jnp.concatenate([half[part * HALF : (part + 1) * HALF] for half in (low, high)], axis=0)
        for part in range(2)
    ]


def add_gram(focal, turned, real, cross):
    real += jnp.dot(turned[0], focal[0], preferred_element_type=jnp.float32)
    real += jnp.dot(turned[1], focal[1], preferred_element_type=jnp.float32)
    cross += jnp.dot(turned[0], focal[1], preferred_element_type=jnp.float32)
    return real, cross


def split(group, turned):
    low, high = turned[:, :HALF], turned[:, HALF:]
    return jnp.where(group == 0, low, high), jnp.where(group == 0, high, low)


def focal_kernel(group_ref, pieces_ref, table_ref, keep_ref, send_ref, real_ref, cross_ref):
    focal = focal_column(pieces_ref, table_ref, 0)
    turned = [focal[part].T for part in range(2)]
    for part in range(2):
        keep_ref[part], send_ref[part] = split(group_ref[0], turned[part])
    zero = jnp.zeros((STACK, STACK), jnp.float32)
    real_ref[...], cross_ref[...] = add_gram(focal, turned, zero, zero)


def more_focal_kernel(
    group_ref, pieces_ref, table_ref, real_ref, cross_ref, keep_ref, second_ref, third_hbm, gram_ref,
    third_ref, third_sem,
):
    real, cross = real_ref[...], cross_ref[...]
    for i in range(1, COLS):
        focal = focal_column(pieces_ref, table_ref, i)
        turned = [focal[part].T for part in range(2)]
        for part in range(2):
            at = (i - 1) * 2 + part
            kept, sent = split(group_ref[0], turned[part])
            keep_ref[at] = kept
            if at < THIRD:
                third_ref[at] = sent
            else:
                second_ref[at - THIRD] = sent
        if i * 2 == THIRD:
            late = pltpu.make_async_copy(third_ref, third_hbm, third_sem)
            late.start()
        real, cross = add_gram(focal, turned, real, cross)
    imag = cross - cross.T
    row = lax.broadcasted_iota(jnp.int32, (STACK, STACK), 0)
    column = lax.broadcasted_iota(jnp.int32, (STACK, STACK), 1)
    packed = jnp.where(row <= column, real, imag)
    for q in range(4):
        top, left = (q // 2) * 128, (q % 2) * 128
        gram_ref[pl.ds(q, 128, stride=4), :] = packed[top : top + 128, left : left + 128]
    late.wait()


def total_kernel(parts_ref, out_ref):
    total = jnp.sum(parts_ref[...].reshape(DEVICES // 2, 8, 128), axis=0)
    total = total[:4] + total[4:]
    twice = jnp.concatenate([total, total], axis=0)
    out_ref[...] = jnp.broadcast_to(twice[None], (DEVICES // 2, 8, 128)).reshape(4 * DEVICES, 128)


def power_kernel(gram_ref, start_ref, left_ref, scale_ref, power_ref):
    quads = [gram_ref[pl.ds(q, 128, stride=4), :] for q in range(4)]
    packed = jnp.concatenate(
        [jnp.concatenate(quads[:2], axis=1), jnp.concatenate(quads[2:], axis=1)], axis=0
    )
    turned = packed.T
    row = lax.broadcasted_iota(jnp.int32, (STACK, STACK), 0)
    column = lax.broadcasted_iota(jnp.int32, (STACK, STACK), 1)
    gram_re = jnp.where(row <= column, packed, turned)
    gram_im = jnp.where(row > column, packed, jnp.where(row == column, 0.0, -turned))
    gram = jnp.concatenate([gram_re, gram_im], axis=0)

    def pieces(value):
        first = value.astype(jnp.bfloat16)
        rest = value - first.astype(jnp.float32)
        second = rest.astype(jnp.bfloat16)
        return first, second, (rest - second.astype(jnp.float32)).astype(jnp.bfloat16)

    grams = pieces(gram)
    left = jnp.concatenate([grams[k] for k in (0, 1, 2, 0, 1, 0)], axis=1)

    def apply(re, im):
        both = jnp.concatenate([re, im], axis=1)
        if both.dtype == jnp.bfloat16:
            right = jnp.concatenate([both] * 3, axis=0)
        else:
            right = pieces(both)
            right = jnp.concatenate([right[k] for k in (0, 0, 0, 1, 1, 2)], axis=0)
        both = jnp.dot(left[:, : right.shape[0]], right, preferred_element_type=jnp.float32)
        return (
            both[:STACK, :RANK] - both[STACK:, RANK:],
            both[:STACK, RANK:] + both[STACK:, :RANK],
        )

    basis_re, basis_im = start_ref[0], start_ref[1]
    for _ in range(STEPS):
        image_re, image_im = apply(basis_re, basis_im)
        norm = jnp.sqrt(
            jnp.sum(image_re * image_re + image_im * image_im, axis=0, keepdims=True) + 1e-06
        )
        basis_re = image_re / norm
        basis_im = image_im / norm
    rounded_re = basis_re.astype(jnp.bfloat16)
    rounded_im = basis_im.astype(jnp.bfloat16)
    image_re, image_im = apply(rounded_re, rounded_im)
    rounded_re = rounded_re.astype(jnp.float32)
    rounded_im = rounded_im.astype(jnp.float32)
    energy = jnp.sum(rounded_re * image_re + rounded_im * image_im, axis=0, keepdims=True)
    trace = jnp.sum(jnp.where(row == column, packed, 0.0))
    power_ref[...] = energy * STACK / trace
    inverse = lax.rsqrt(energy / (NROW * NCOL) + 1e-06)
    scale_ref[...] = jnp.broadcast_to(inverse, (RANK, RANK)).T
    turned_re = rounded_re.T.astype(jnp.bfloat16)
    turned_im = rounded_im.T.astype(jnp.bfloat16)
    left_ref[:RANK, :STACK] = turned_re
    left_ref[:RANK, STACK:] = -turned_im
    left_ref[RANK:, :STACK] = turned_im
    left_ref[RANK:, STACK:] = turned_re


def modes_kernel(
    group_ref, left_ref, scale_ref, kept_ref, kept_more_ref, first_ref, second_ref, third_ref,
    out_hbm,    wide_ref, out_ref, out_sem,
):
    group = group_ref[0]
    left = left_ref[...]
    scale = scale_ref[...]
    sources = (
        [kept_ref[part] for part in range(2)] + [kept_more_ref[at] for at in range(2 * COLS - 2)],
        [first_ref[part] for part in range(2)]
        + [third_ref[at] for at in range(THIRD)]
        + [second_ref[at] for at in range(2 * COLS - 2 - THIRD)],
    )
    for source in range(2):
        first = jnp.where(group == source, 0, COLS)
        for i in range(COLS):
            focal = jnp.concatenate(sources[source][2 * i : 2 * i + 2], axis=0)
            mode = jnp.dot(left, focal, preferred_element_type=jnp.float32)
            for part in range(2):
                for lane in range(HALF // 128):
                    rows = pl.ds(
                        (part * 2 + lane) * WIDE + first + i, RANK, stride=GROUPS * COLS
                    )
                    wide_ref[rows, :] = (
                        mode[part * RANK : (part + 1) * RANK, lane * 128 : (lane + 1) * 128] * scale
                    )
    copies = []
    for part in range(2):
        for lane in range(HALF // 128):
            at = (part * 2 + lane) * WIDE
            out_ref[part, :, :, lane * 128 : (lane + 1) * 128] = (
                wide_ref[at : at + WIDE, :].reshape(RANK, GROUPS * COLS, 128).astype(jnp.bfloat16)
            )
        copies.append(pltpu.make_async_copy(out_ref.at[part], out_hbm.at[part], out_sem.at[part]))
        copies[-1].start()
    for copy in copies:
        copy.wait()


VMEM = pl.BlockSpec(memory_space=pltpu.VMEM)
HBM = pl.BlockSpec(memory_space=pltpu.HBM)
SMEM = pl.BlockSpec(memory_space=pltpu.SMEM)


def params(mib):
    return pltpu.CompilerParams(vmem_limit_bytes=mib * 1024 * 1024)


def local(fields, lens_phase, occupancy, focus_scale, assignment, start_basis):
    group = lax.axis_index("grp").astype(jnp.int32).reshape(1)
    column_table = jnp.asarray(column_tables())
    across = pl.pallas_call(
        spectra_kernel,
        out_shape=jax.ShapeDtypeStruct((DEVICES, COLS, 2 * ROWS, SLOTS), jnp.bfloat16),
        in_specs=[SMEM] + [HBM] * 6,
        out_specs=VMEM,
        scratch_shapes=[
            pltpu.SMEM((STACK,), jnp.int32),
            pltpu.SMEM((STACK,), jnp.float32),
            pltpu.SMEM((STACK,), jnp.float32),
            pltpu.VMEM((2, SLOTS, ROWS, NCOL), jnp.bfloat16),
            pltpu.VMEM((ROWS, NCOL), jnp.float32),
            pltpu.VMEM((2, NCOL, NCOL), jnp.bfloat16),
            pltpu.VMEM((NCOL // 128 * ROWS * SLOTS, 128), jnp.float32),
            pltpu.VMEM((NCOL // 128 * ROWS * SLOTS, 128), jnp.float32),
            pltpu.VMEM((2 * ROWS * PLANE, SLOTS), jnp.float32),
            pltpu.SemaphoreType.DMA((4,)),
            pltpu.SemaphoreType.DMA((2, CHUNKS)),
            pltpu.SemaphoreType.DMA((2,)),
        ],
        compiler_params=params(24),
        name="spectra",
    )(
        group,
        *(
            pltpu.with_memory_space_constraint(array, pltpu.HBM)
            for array in (
                assignment, occupancy, focus_scale, fields[0], lens_phase, column_table
            )
        ),
    )
    pieces = lax.all_to_all(across, AXES, 0, 0, tiled=True)
    pieces = pieces.reshape(DEVICES, COLS, 2, ROWS, SLOTS)


    def focal_shape(count):
        return jax.ShapeDtypeStruct((count, STACK, HALF), jnp.bfloat16)

    row_table = jnp.asarray(row_tables())
    square = jax.ShapeDtypeStruct((STACK, STACK), jnp.float32)
    kept, swap_first, real, cross = pl.pallas_call(
        focal_kernel,
        out_shape=(focal_shape(2), focal_shape(2), square, square),
        in_specs=[SMEM] + [VMEM] * 2,
        out_specs=(VMEM,) * 4,
        compiler_params=params(12),
        name="focal",
    )(group, pieces, row_table)
    kept_more, swap_second, swap_third, gram = pl.pallas_call(
        more_focal_kernel,
        out_shape=(
            focal_shape(2 * COLS - 2),
            focal_shape(2 * COLS - 2 - THIRD),
            pltpu.HBM((THIRD, STACK, HALF), jnp.bfloat16),
            jax.ShapeDtypeStruct((4 * DEVICES, 128), jnp.float32),
        ),
        in_specs=[SMEM] + [VMEM] * 4,
        out_specs=(VMEM, VMEM, HBM, VMEM),
        scratch_shapes=[pltpu.VMEM((THIRD, STACK, HALF), jnp.bfloat16), pltpu.SemaphoreType.DMA],
        compiler_params=params(12),
        name="more_focal",
    )(group, pieces, row_table, real, cross)
    swap_first = lax.ppermute(swap_first, "grp", [(0, 1), (1, 0)])
    swap_second = lax.ppermute(swap_second, "grp", [(0, 1), (1, 0)])
    swap_third = lax.ppermute(swap_third, "grp", [(0, 1), (1, 0)])
    parts = lax.all_to_all(gram.reshape(DEVICES, 4, 128), AXES, 0, 0, tiled=True)
    total = pl.pallas_call(
        total_kernel,
        out_shape=jax.ShapeDtypeStruct((4 * DEVICES, 128), jnp.float32),
        in_specs=[VMEM],
        out_specs=VMEM,
        compiler_params=params(4),
        name="total",
    )(parts.reshape(4 * DEVICES, 128))
    whole = lax.all_to_all(total.reshape(DEVICES, 4, 128), AXES, 0, 0, tiled=True)
    left, scale, power = pl.pallas_call(
        power_kernel,
        out_shape=(
            jax.ShapeDtypeStruct((2 * RANK, 2 * STACK), jnp.bfloat16),
            jax.ShapeDtypeStruct((RANK, RANK), jnp.float32),
            jax.ShapeDtypeStruct((1, RANK), jnp.float32),
        ),
        in_specs=[VMEM] * 2,
        out_specs=(VMEM,) * 3,
        compiler_params=params(12),
        name="power",
    )(whole.reshape(4 * DEVICES, 128), start_basis)
    coherent_modes = pl.pallas_call(
        modes_kernel,
        out_shape=jax.ShapeDtypeStruct((2, RANK, GROUPS * COLS, HALF), jnp.bfloat16),
        in_specs=[SMEM] + [VMEM] * 7,
        out_specs=HBM,
        scratch_shapes=[
            pltpu.VMEM((2 * HALF // 128 * WIDE, 128), jnp.float32),
            pltpu.VMEM((2, RANK, GROUPS * COLS, HALF), jnp.bfloat16),
            pltpu.SemaphoreType.DMA((2,)),
        ],
        compiler_params=params(16),
        name="modes",
    )(group, left, scale, kept, kept_more, swap_first, swap_second, swap_third)
    return coherent_modes, power.reshape(RANK)


def solution(mesh):
    in_specs = (P("grp", None, None, "pix", None), P("pix", None), P(), P(), P(), P())
    out_specs = (P(None, None, "pix", "grp"), P())

    return jax.shard_map(local, mesh=mesh, in_specs=in_specs, out_specs=out_specs, check_vma=False)
```

```python
import math

import jax
import jax.numpy as jnp
import numpy as np
from jax import lax
from jax.experimental import pallas as pl
from jax.experimental.pallas import tpu as pltpu
from jax.sharding import PartitionSpec as P

NROW = 512
NCOL = 512
STEPS = 2
GROUPS = 2
PIX = 64
DEVICES = GROUPS * PIX
SLOTS = 128
STACK = GROUPS * SLOTS
RANK = 128
ROWS = NROW // PIX
COLS = NCOL // DEVICES
HALF = NROW // GROUPS
WIDE = RANK * GROUPS * COLS
FIRST = 3
CHUNKS = 4
CHUNK = SLOTS // CHUNKS
PLANE = DEVICES * COLS + 1
AXES = ("grp", "pix")

LIMIT = 0.5 * 1.5 * 3.140625


def fit(function, terms):
    limit = LIMIT * 1.001
    nodes = np.cos(np.pi * (np.arange(400) + 0.5) / 400)
    square = (nodes + 1.0) * 0.5 * limit * limit
    powers = np.stack([square**k for k in range(terms)], axis=1)
    return [float(c) for c in np.linalg.lstsq(powers, function(np.sqrt(square)), rcond=None)[0]]


SIN_FIT = fit(lambda x: np.sin(x) / x, 6)
COS_FIT = fit(np.cos, 6)


def tables(length):
    index = np.arange(length, dtype=np.int64)
    angle = (index[:, None] * index[None, :] % length).astype(np.float32) * np.float32(
        2.0 * math.pi / length
    )
    factor = np.float32(1.0 / math.sqrt(length))
    cosine = (np.cos(angle) * factor).astype(jnp.bfloat16)
    sine = (np.sin(angle) * factor).astype(jnp.bfloat16)
    return cosine, sine


def column_tables():
    i, g, p = np.meshgrid(
        np.arange(COLS), np.arange(GROUPS), np.arange(PIX // 2), indexing="ij"
    )
    order = (p * (GROUPS * COLS) + g * COLS + i).reshape(-1)
    pair = np.arange(0, NCOL, 256)[:, None]
    lane = np.arange(64)
    even = np.concatenate([pair + 2 * lane, pair + 128 + 2 * lane], axis=1).reshape(-1)
    odd = np.concatenate([pair + 129 + 2 * lane, pair + 1 + 2 * lane], axis=1).reshape(-1)
    cosine, sine = (table[order] for table in tables(NCOL))
    return np.stack(
        [
            np.block([[cosine[:, k], sine[:, k]], [-sine[:, k], cosine[:, k]]])
            for k in (even, odd)
        ]
    )


def row_tables():
    cosine, sine = (
        table[:HALF].reshape(HALF, PIX, ROWS // 2, 2).transpose(3, 0, 1, 2)
        for table in tables(NROW)
    )
    real = np.stack([cosine, sine], axis=3).reshape(2, HALF, NROW)
    imag = np.stack([-sine, cosine], axis=3).reshape(2, HALF, NROW)
    return np.concatenate([real, imag], axis=1)


def polynomial(square, coefficients):
    total = square * coefficients[-1] + coefficients[-2]
    for coefficient in coefficients[-3::-1]:
        total = total * square + coefficient
    return total


def spectra_kernel(
    group_ref, assign_hbm, occ_hbm, chrom_hbm, fields_hbm, lens_hbm, table_hbm, out_ref,
    assign_ref, occ_ref, chrom_ref, fields_ref, lens_ref, table_ref,
    real_ref, imag_ref, wide_ref, small_sem, field_sem, table_sem,
):
    def chunk(part, c):
        slots = pl.ds(c * CHUNK, CHUNK)
        return pltpu.make_async_copy(
            fields_hbm.at[part, slots], fields_ref.at[part, slots], field_sem.at[part, c]
        )

    small = [
        pltpu.make_async_copy(source, target, small_sem.at[k])
        for k, (source, target) in enumerate(
            (
                (assign_hbm, assign_ref),
                (occ_hbm, occ_ref),
                (chrom_hbm, chrom_ref),
                (lens_hbm, lens_ref),
            )
        )
    ]
    large = [
        pltpu.make_async_copy(table_hbm.at[odd], table_ref.at[odd], table_sem.at[odd])
        for odd in range(2)
    ]
    for copy in small:
        copy.start()
    for c in range(CHUNKS):
        for part in range(2):
            chunk(part, c).start()
    for copy in large:
        copy.start()
    for copy in small:
        copy.wait()
    base = group_ref[0] * SLOTS

    def phase(m, carry):
        electron = assign_ref[base + m]
        amplitude = jnp.sqrt(jnp.full((ROWS, 128), occ_ref[electron], jnp.float32))
        twice = amplitude + amplitude
        chromatic = chrom_ref[electron] * 0.5
        for lane in range(NCOL // 128):
            cut = pl.ds(lane * 128, 128)
            half = lens_ref[:, cut] * chromatic
            square = half * half
            sine_half = half * polynomial(square, SIN_FIT)
            scaled = sine_half * twice
            sine = scaled * polynomial(square, COS_FIT)
            cosine = amplitude - scaled * sine_half
            field_re = fields_ref[0, m, :, cut].astype(jnp.float32)
            field_im = fields_ref[1, m, :, cut].astype(jnp.float32)
            rows = pl.ds(pl.multiple_of(lane * ROWS * SLOTS + m * ROWS, ROWS), ROWS)
            real_ref[rows, :] = field_re * cosine - field_im * sine
            imag_ref[rows, :] = field_re * sine + field_im * cosine
        return carry

    for c in range(CHUNKS):
        for part in range(2):
            chunk(part, c).wait()
        lax.fori_loop(c * CHUNK, (c + 1) * CHUNK, phase, 0, unroll=16)
    for copy in large:
        copy.wait()
    lane = lax.broadcasted_iota(jnp.int32, (SLOTS, 128), 1)
    evens_first = 2 * (lane % 64) + lane // 64
    odds_first = 2 * (lane % 64) + 1 - lane // 64

    def parts(ref, j):
        even, odd = [], []
        for tile in range(0, NCOL // 128, 2):
            left, right = (
                ref[pl.ds((tile + k) * ROWS * SLOTS + j, SLOTS, stride=ROWS), :] for k in range(2)
            )
            left = jnp.take_along_axis(left, evens_first, axis=1)
            right = jnp.take_along_axis(right, odds_first, axis=1)
            even.append(jnp.where(lane < 64, left, right))
            odd.append(jnp.where(lane < 64, right, left))
        return even, odd

    contract = (((1,), (1,)), ((), ()))
    for j in range(0, ROWS, 2):
        waves = [[], []]
        for q in range(2):
            real, imag = parts(real_ref, j + q), parts(imag_ref, j + q)
            for odd in range(2):
                waves[odd].append(jnp.concatenate(real[odd] + imag[odd], axis=1))
        even, odd = (
            lax.dot_general(
                table_ref[k],
                jnp.concatenate(waves[k], axis=0).astype(jnp.bfloat16),
                contract,
                preferred_element_type=jnp.float32,
            )
            for k in range(2)
        )
        for half, across in ((0, even + odd), (1, even - odd)):
            for q in range(2):
                for part in range(2):
                    for block in range(COLS * GROUPS):
                        i, g = block // GROUPS, block % GROUPS
                        device = g * PIX + half * (PIX // 2)
                        at = q * ROWS + part * (ROWS // 2) + j // 2
                        row = part * (NCOL // 2) + block * (PIX // 2)
                        wide_ref[pl.ds(at * PLANE + i * DEVICES + device, PIX // 2), :] = across[
                            row : row + PIX // 2, q * SLOTS : (q + 1) * SLOTS
                        ]
    for i in range(COLS):

        def gather(d, carry):
            rows = wide_ref[pl.ds(i * DEVICES + d, 2 * ROWS, stride=PLANE), :]
            out_ref[d, i] = rows.astype(jnp.bfloat16)
            return carry

        lax.fori_loop(0, DEVICES, gather, 0, unroll=8)


def focal_column(pieces_ref, table_ref, i):
    halves = []
    for odd in range(2):
        wave = jnp.concatenate(
            [
                pieces_ref[g * PIX : (g + 1) * PIX, i, odd].reshape(NROW, SLOTS)
                for g in range(GROUPS)
            ],
            axis=1,
        )
        halves.append(jnp.dot(table_ref[odd], wave, preferred_element_type=jnp.float32))
    low = (halves[0] + halves[1]).astype(jnp.bfloat16)
    high = (halves[0] - halves[1]).astype(jnp.bfloat16)
    return [
        jnp.concatenate([half[part * HALF : (part + 1) * HALF] for half in (low, high)], axis=0)
        for part in range(2)
    ]


def add_gram(focal, turned, real, cross):
    real += jnp.dot(turned[0], focal[0], preferred_element_type=jnp.float32)
    real += jnp.dot(turned[1], focal[1], preferred_element_type=jnp.float32)
    cross += jnp.dot(turned[0], focal[1], preferred_element_type=jnp.float32)
    return real, cross


def split(group, turned):
    low, high = turned[:, :HALF], turned[:, HALF:]
    return jnp.where(group == 0, low, high), jnp.where(group == 0, high, low)


def focal_kernel(
    group_ref, pieces_ref, table_ref, keep_ref, first_ref, second_ref, gram_ref
):
    real = jnp.zeros((STACK, STACK), jnp.float32)
    cross = jnp.zeros((STACK, STACK), jnp.float32)
    for i in range(COLS):
        focal = focal_column(pieces_ref, table_ref, i)
        turned = [focal[part].T for part in range(2)]
        for part in range(2):
            at = 2 * i + part
            keep_ref[at], sent = split(group_ref[0], turned[part])
            if at < FIRST:
                first_ref[at] = sent
            else:
                second_ref[at - FIRST] = sent
        real, cross = add_gram(focal, turned, real, cross)
    imag = cross - cross.T
    row = lax.broadcasted_iota(jnp.int32, (STACK, STACK), 0)
    column = lax.broadcasted_iota(jnp.int32, (STACK, STACK), 1)
    packed = jnp.where(row <= column, real, imag)
    for q in range(4):
        top, left = (q // 2) * 128, (q % 2) * 128
        gram_ref[pl.ds(q, 128, stride=4), :] = packed[top : top + 128, left : left + 128]


def total_kernel(parts_ref, out_ref):
    total = jnp.sum(parts_ref[...].reshape(DEVICES // 2, 8, 128), axis=0)
    total = total[:4] + total[4:]
    twice = jnp.concatenate([total, total], axis=0)
    out_ref[...] = jnp.broadcast_to(twice[None], (DEVICES // 2, 8, 128)).reshape(4 * DEVICES, 128)


def power_kernel(gram_ref, start_ref, left_ref, scale_ref, power_ref):
    quads = [gram_ref[pl.ds(q, 128, stride=4), :] for q in range(4)]
    packed = jnp.concatenate(
        [jnp.concatenate(quads[:2], axis=1), jnp.concatenate(quads[2:], axis=1)], axis=0
    )
    turned = packed.T
    row = lax.broadcasted_iota(jnp.int32, (STACK, STACK), 0)
    column = lax.broadcasted_iota(jnp.int32, (STACK, STACK), 1)
    gram_re = jnp.where(row <= column, packed, turned)
    gram_im = jnp.where(row > column, packed, jnp.where(row == column, 0.0, -turned))
    gram = jnp.concatenate([gram_re, gram_im], axis=0)

    def pieces(value):
        first = value.astype(jnp.bfloat16)
        rest = value - first.astype(jnp.float32)
        second = rest.astype(jnp.bfloat16)
        return first, second, (rest - second.astype(jnp.float32)).astype(jnp.bfloat16)

    grams = pieces(gram)
    left = jnp.concatenate([grams[k] for k in (0, 1, 2, 0, 1, 0)], axis=1)

    def apply(re, im):
        both = jnp.concatenate([re, im], axis=1)
        if both.dtype == jnp.bfloat16:
            right = jnp.concatenate([both] * 3, axis=0)
        else:
            right = pieces(both)
            right = jnp.concatenate([right[k] for k in (0, 0, 0, 1, 1, 2)], axis=0)
        both = jnp.dot(left[:, : right.shape[0]], right, preferred_element_type=jnp.float32)
        return (
            both[:STACK, :RANK] - both[STACK:, RANK:],
            both[:STACK, RANK:] + both[STACK:, :RANK],
        )

    basis_re, basis_im = start_ref[0], start_ref[1]
    for _ in range(STEPS):
        image_re, image_im = apply(basis_re, basis_im)
        norm = jnp.sqrt(
            jnp.sum(image_re * image_re + image_im * image_im, axis=0, keepdims=True) + 1e-06
        )
        basis_re = image_re / norm
        basis_im = image_im / norm
    rounded_re = basis_re.astype(jnp.bfloat16)
    rounded_im = basis_im.astype(jnp.bfloat16)
    image_re, image_im = apply(rounded_re, rounded_im)
    rounded_re = rounded_re.astype(jnp.float32)
    rounded_im = rounded_im.astype(jnp.float32)
    energy = jnp.sum(rounded_re * image_re + rounded_im * image_im, axis=0, keepdims=True)
    trace = jnp.sum(jnp.where(row == column, packed, 0.0))
    power_ref[...] = energy * STACK / trace
    inverse = lax.rsqrt(energy / (NROW * NCOL) + 1e-06)
    scale_ref[...] = jnp.broadcast_to(inverse, (RANK, RANK)).T
    turned_re = rounded_re.T.astype(jnp.bfloat16)
    turned_im = rounded_im.T.astype(jnp.bfloat16)
    left_ref[:RANK, :STACK] = turned_re
    left_ref[:RANK, STACK:] = -turned_im
    left_ref[RANK:, :STACK] = turned_im
    left_ref[RANK:, STACK:] = turned_re


def modes_kernel(
    group_ref, left_ref, scale_ref, kept_ref, first_ref, second_ref, out_hbm,
       wide_ref, out_ref, out_sem,
):
    group = group_ref[0]
    left = left_ref[...]
    scale = scale_ref[...]
    sources = (
        [kept_ref[at] for at in range(2 * COLS)],
        [first_ref[at] for at in range(FIRST)]
        + [second_ref[at] for at in range(2 * COLS - FIRST)],
    )
    for source in range(2):
        first = jnp.where(group == source, 0, COLS)
        for i in range(COLS):
            focal = jnp.concatenate(sources[source][2 * i : 2 * i + 2], axis=0)
            mode = jnp.dot(left, focal, preferred_element_type=jnp.float32)
            for part in range(2):
                for lane in range(HALF // 128):
                    rows = pl.ds(
                        (part * 2 + lane) * WIDE + first + i, RANK, stride=GROUPS * COLS
                    )
                    wide_ref[rows, :] = (
                        mode[part * RANK : (part + 1) * RANK, lane * 128 : (lane + 1) * 128] * scale
                    )
    copies = []
    for part in range(2):
        for lane in range(HALF // 128):
            at = (part * 2 + lane) * WIDE
            out_ref[part, :, :, lane * 128 : (lane + 1) * 128] = (
                wide_ref[at : at + WIDE, :].reshape(RANK, GROUPS * COLS, 128).astype(jnp.bfloat16)
            )
        copies.append(pltpu.make_async_copy(out_ref.at[part], out_hbm.at[part], out_sem.at[part]))
        copies[-1].start()
    for copy in copies:
        copy.wait()


VMEM = pl.BlockSpec(memory_space=pltpu.VMEM)
HBM = pl.BlockSpec(memory_space=pltpu.HBM)
SMEM = pl.BlockSpec(memory_space=pltpu.SMEM)


def params(mib):
    return pltpu.CompilerParams(vmem_limit_bytes=mib * 1024 * 1024)


def local(fields, lens_phase, occupancy, focus_scale, assignment, start_basis):
    group = lax.axis_index("grp").astype(jnp.int32).reshape(1)
    column_table = jnp.asarray(column_tables())
    across = pl.pallas_call(
        spectra_kernel,
        out_shape=jax.ShapeDtypeStruct((DEVICES, COLS, 2 * ROWS, SLOTS), jnp.bfloat16),
        in_specs=[SMEM] + [HBM] * 6,
        out_specs=VMEM,
        scratch_shapes=[
            pltpu.SMEM((STACK,), jnp.int32),
            pltpu.SMEM((STACK,), jnp.float32),
            pltpu.SMEM((STACK,), jnp.float32),
            pltpu.VMEM((2, SLOTS, ROWS, NCOL), jnp.bfloat16),
            pltpu.VMEM((ROWS, NCOL), jnp.float32),
            pltpu.VMEM((2, NCOL, NCOL), jnp.bfloat16),
            pltpu.VMEM((NCOL // 128 * ROWS * SLOTS, 128), jnp.float32),
            pltpu.VMEM((NCOL // 128 * ROWS * SLOTS, 128), jnp.float32),
            pltpu.VMEM((2 * ROWS * PLANE, SLOTS), jnp.float32),
            pltpu.SemaphoreType.DMA((4,)),
            pltpu.SemaphoreType.DMA((2, CHUNKS)),
            pltpu.SemaphoreType.DMA((2,)),
        ],
        compiler_params=params(24),
        name="spectra",
    )(
        group,
        *(
            pltpu.with_memory_space_constraint(array, pltpu.HBM)
            for array in (
                assignment, occupancy, focus_scale, fields[0], lens_phase, column_table
            )
        ),
    )
    pieces = lax.all_to_all(across, AXES, 0, 0, tiled=True)
    pieces = pieces.reshape(DEVICES, COLS, 2, ROWS, SLOTS)


    def focal_shape(count):
        return jax.ShapeDtypeStruct((count, STACK, HALF), jnp.bfloat16)

    kept, swap_first, swap_second, gram = pl.pallas_call(
        focal_kernel,
        out_shape=(
            focal_shape(2 * COLS),
            focal_shape(FIRST),
            focal_shape(2 * COLS - FIRST),
            jax.ShapeDtypeStruct((4 * DEVICES, 128), jnp.float32),
        ),
        in_specs=[SMEM] + [VMEM] * 2,
        out_specs=(VMEM,) * 4,
        compiler_params=params(12),
        name="focal",
    )(group, pieces, jnp.asarray(row_tables()))
    swap_first = lax.ppermute(swap_first, "grp", [(0, 1), (1, 0)])
    swap_second = lax.ppermute(swap_second, "grp", [(0, 1), (1, 0)])
    parts = lax.all_to_all(gram.reshape(DEVICES, 4, 128), AXES, 0, 0, tiled=True)
    total = pl.pallas_call(
        total_kernel,
        out_shape=jax.ShapeDtypeStruct((4 * DEVICES, 128), jnp.float32),
        in_specs=[VMEM],
        out_specs=VMEM,
        compiler_params=params(4),
        name="total",
    )(parts.reshape(4 * DEVICES, 128))
    whole = lax.all_to_all(total.reshape(DEVICES, 4, 128), AXES, 0, 0, tiled=True)
    left, scale, power = pl.pallas_call(
        power_kernel,
        out_shape=(
            jax.ShapeDtypeStruct((2 * RANK, 2 * STACK), jnp.bfloat16),
            jax.ShapeDtypeStruct((RANK, RANK), jnp.float32),
            jax.ShapeDtypeStruct((1, RANK), jnp.float32),
        ),
        in_specs=[VMEM] * 2,
        out_specs=(VMEM,) * 3,
        compiler_params=params(12),
        name="power",
    )(whole.reshape(4 * DEVICES, 128), start_basis)
    coherent_modes = pl.pallas_call(
        modes_kernel,
        out_shape=jax.ShapeDtypeStruct((2, RANK, GROUPS * COLS, HALF), jnp.bfloat16),
        in_specs=[SMEM] + [VMEM] * 5,
        out_specs=HBM,
        scratch_shapes=[
            pltpu.VMEM((2 * HALF // 128 * WIDE, 128), jnp.float32),
            pltpu.VMEM((2, RANK, GROUPS * COLS, HALF), jnp.bfloat16),
            pltpu.SemaphoreType.DMA((2,)),
        ],
        compiler_params=params(16),
        name="modes",
    )(group, left, scale, kept, swap_first, swap_second)
    return coherent_modes, power.reshape(RANK)


def solution(mesh):
    in_specs = (P("grp", None, None, "pix", None), P("pix", None), P(), P(), P(), P())
    out_specs = (P(None, None, "pix", "grp"), P())

    return jax.shard_map(local, mesh=mesh, in_specs=in_specs, out_specs=out_specs, check_vma=False)
```

```python
import math

import jax
import jax.numpy as jnp
import numpy as np
from jax import lax
from jax.experimental import pallas as pl
from jax.experimental.pallas import tpu as pltpu
from jax.sharding import PartitionSpec as P

NROW = 512
NCOL = 512
STEPS = 2
GROUPS = 2
PIX = 64
DEVICES = GROUPS * PIX
SLOTS = 128
STACK = GROUPS * SLOTS
RANK = 128
ROWS = NROW // PIX
COLS = NCOL // DEVICES
HALF = NROW // GROUPS
WIDE = RANK * GROUPS * COLS
FIRST = 3
CHUNKS = 4
CHUNK = SLOTS // CHUNKS
PLANE = DEVICES * COLS + 1
AXES = ("grp", "pix")

LENS = 3.140625
SCALE_LOW, SCALE_HIGH = 0.5, 1.5
STEP = 0.125
BASES = int((SCALE_HIGH - SCALE_LOW) / STEP) + 1


def fit(function, terms, limit):
    nodes = np.cos(np.pi * (np.arange(400) + 0.5) / 400)
    square = (nodes + 1.0) * 0.5 * (limit * 1.001) ** 2
    powers = np.stack([square**k for k in range(terms)], axis=1)
    return [float(c) for c in np.linalg.lstsq(powers, function(np.sqrt(square)), rcond=None)[0]]


SIN_FIT = fit(lambda x: np.sin(x) / x, 6, 0.5 * SCALE_HIGH * LENS)
COS_FIT = fit(np.cos, 7, 0.5 * SCALE_HIGH * LENS)
SIN_REST = fit(lambda x: np.sin(x) / x, 3, 0.5 * STEP * LENS)
COS_REST = fit(np.cos, 3, 0.5 * STEP * LENS)


def tables(length):
    index = np.arange(length, dtype=np.int64)
    angle = (index[:, None] * index[None, :] % length).astype(np.float32) * np.float32(
        2.0 * math.pi / length
    )
    factor = np.float32(1.0 / math.sqrt(length))
    cosine = (np.cos(angle) * factor).astype(jnp.bfloat16)
    sine = (np.sin(angle) * factor).astype(jnp.bfloat16)
    return cosine, sine


def column_tables():
    i, g, p = np.meshgrid(
        np.arange(COLS), np.arange(GROUPS), np.arange(PIX // 2), indexing="ij"
    )
    order = (p * (GROUPS * COLS) + g * COLS + i).reshape(-1)
    pair = np.arange(0, NCOL, 256)[:, None]
    lane = np.arange(64)
    even = np.concatenate([pair + 2 * lane, pair + 128 + 2 * lane], axis=1).reshape(-1)
    odd = np.concatenate([pair + 129 + 2 * lane, pair + 1 + 2 * lane], axis=1).reshape(-1)
    cosine, sine = (table[order] for table in tables(NCOL))
    return np.stack(
        [
            np.block([[cosine[:, k], sine[:, k]], [-sine[:, k], cosine[:, k]]])
            for k in (even, odd)
        ]
    )


def row_tables():
    cosine, sine = (
        table[:HALF].reshape(HALF, PIX, ROWS // 2, 2).transpose(3, 0, 1, 2)
        for table in tables(NROW)
    )
    real = np.stack([cosine, sine], axis=3).reshape(2, HALF, NROW)
    imag = np.stack([-sine, cosine], axis=3).reshape(2, HALF, NROW)
    return np.concatenate([real, imag], axis=1)


def polynomial(square, coefficients):
    total = square * coefficients[-1] + coefficients[-2]
    for coefficient in coefficients[-3::-1]:
        total = total * square + coefficient
    return total


def spectra_kernel(
    group_ref, assign_hbm, occ_hbm, chrom_hbm, fields_hbm, lens_hbm, table_hbm, out_ref,
    assign_ref, occ_ref, chrom_ref, fields_ref, lens_ref, table_ref,
    base_ref, real_ref, imag_ref, wide_ref, small_sem, field_sem, table_sem,
):
    def chunk(part, c):
        slots = pl.ds(c * CHUNK, CHUNK)
        return pltpu.make_async_copy(
            fields_hbm.at[part, slots], fields_ref.at[part, slots], field_sem.at[part, c]
        )

    small = [
        pltpu.make_async_copy(source, target, small_sem.at[k])
        for k, (source, target) in enumerate(
            (
                (assign_hbm, assign_ref),
                (occ_hbm, occ_ref),
                (chrom_hbm, chrom_ref),
                (lens_hbm, lens_ref),
            )
        )
    ]
    large = [
        pltpu.make_async_copy(table_hbm.at[odd], table_ref.at[odd], table_sem.at[odd])
        for odd in range(2)
    ]
    for copy in small:
        copy.start()
    for c in range(CHUNKS):
        for part in range(2):
            chunk(part, c).start()
    for copy in large:
        copy.start()
    for copy in small:
        copy.wait()
    base = group_ref[0] * SLOTS

    def base_wave(k, carry):
        scale = 0.5 * (SCALE_LOW + STEP * k.astype(jnp.float32))
        for lane in range(NCOL // 128):
            cut = pl.ds(lane * 128, 128)
            half = lens_ref[:, cut] * scale
            square = half * half
            sine_half = half * polynomial(square, SIN_FIT)
            double = sine_half + sine_half
            base_ref[k, 0, :, cut] = 1.0 - double * sine_half
            base_ref[k, 1, :, cut] = double * polynomial(square, COS_FIT)
        return carry

    lax.fori_loop(0, BASES, base_wave, 0)

    def phase(m, carry):
        electron = assign_ref[base + m]
        amplitude = jnp.sqrt(jnp.full((ROWS, 128), occ_ref[electron], jnp.float32))
        chromatic = chrom_ref[electron]
        nearest = ((chromatic - SCALE_LOW) * (1.0 / STEP) + 0.5).astype(jnp.int32)
        nearest = jnp.clip(nearest, 0, BASES - 1)
        rest = chromatic - (SCALE_LOW + STEP * nearest.astype(jnp.float32))
        for lane in range(NCOL // 128):
            cut = pl.ds(lane * 128, 128)
            angle = lens_ref[:, cut] * rest
            square = angle * angle
            sine_rest = amplitude * (angle * polynomial(square, SIN_REST))
            cosine_rest = amplitude * polynomial(square, COS_REST)
            cosine_base = base_ref[nearest, 0, :, cut]
            sine_base = base_ref[nearest, 1, :, cut]
            cosine = cosine_base * cosine_rest - sine_base * sine_rest
            sine = sine_base * cosine_rest + cosine_base * sine_rest
            field_re = fields_ref[0, m, :, cut].astype(jnp.float32)
            field_im = fields_ref[1, m, :, cut].astype(jnp.float32)
            rows = pl.ds(pl.multiple_of(lane * ROWS * SLOTS + m * ROWS, ROWS), ROWS)
            real_ref[rows, :] = field_re * cosine - field_im * sine
            imag_ref[rows, :] = field_re * sine + field_im * cosine
        return carry

    for c in range(CHUNKS):
        for part in range(2):
            chunk(part, c).wait()
        lax.fori_loop(c * CHUNK, (c + 1) * CHUNK, phase, 0, unroll=16)
    for copy in large:
        copy.wait()
    lane = lax.broadcasted_iota(jnp.int32, (SLOTS, 128), 1)
    evens_first = 2 * (lane % 64) + lane // 64
    odds_first = 2 * (lane % 64) + 1 - lane // 64

    def parts(ref, j):
        even, odd = [], []
        for tile in range(0, NCOL // 128, 2):
            left, right = (
                ref[pl.ds((tile + k) * ROWS * SLOTS + j, SLOTS, stride=ROWS), :] for k in range(2)
            )
            left = jnp.take_along_axis(left, evens_first, axis=1)
            right = jnp.take_along_axis(right, odds_first, axis=1)
            even.append(jnp.where(lane < 64, left, right))
            odd.append(jnp.where(lane < 64, right, left))
        return even, odd

    contract = (((1,), (1,)), ((), ()))
    for j in range(0, ROWS, 2):
        waves = [[], []]
        for q in range(2):
            real, imag = parts(real_ref, j + q), parts(imag_ref, j + q)
            for odd in range(2):
                waves[odd].append(jnp.concatenate(real[odd] + imag[odd], axis=1))
        even, odd = (
            lax.dot_general(
                table_ref[k],
                jnp.concatenate(waves[k], axis=0).astype(jnp.bfloat16),
                contract,
                preferred_element_type=jnp.float32,
            )
            for k in range(2)
        )
        for half, across in ((0, even + odd), (1, even - odd)):
            for q in range(2):
                for part in range(2):
                    for block in range(COLS * GROUPS):
                        i, g = block // GROUPS, block % GROUPS
                        device = g * PIX + half * (PIX // 2)
                        at = q * ROWS + part * (ROWS // 2) + j // 2
                        row = part * (NCOL // 2) + block * (PIX // 2)
                        wide_ref[pl.ds(at * PLANE + i * DEVICES + device, PIX // 2), :] = across[
                            row : row + PIX // 2, q * SLOTS : (q + 1) * SLOTS
                        ]
    for i in range(COLS):

        def gather(d, carry):
            rows = wide_ref[pl.ds(i * DEVICES + d, 2 * ROWS, stride=PLANE), :]
            out_ref[d, i] = rows.astype(jnp.bfloat16)
            return carry

        lax.fori_loop(0, DEVICES, gather, 0, unroll=DEVICES)


def focal_column(pieces_ref, table_ref, i):
    halves = []
    for odd in range(2):
        wave = jnp.concatenate(
            [
                pieces_ref[g * PIX : (g + 1) * PIX, i, odd].reshape(NROW, SLOTS)
                for g in range(GROUPS)
            ],
            axis=1,
        )
        halves.append(jnp.dot(table_ref[odd], wave, preferred_element_type=jnp.float32))
    low = (halves[0] + halves[1]).astype(jnp.bfloat16)
    high = (halves[0] - halves[1]).astype(jnp.bfloat16)
    return [
        jnp.concatenate([half[part * HALF : (part + 1) * HALF] for half in (low, high)], axis=0)
        for part in range(2)
    ]


def add_gram(focal, turned, real, cross):
    real += jnp.dot(turned[0], focal[0], preferred_element_type=jnp.float32)
    real += jnp.dot(turned[1], focal[1], preferred_element_type=jnp.float32)
    cross += jnp.dot(turned[0], focal[1], preferred_element_type=jnp.float32)
    return real, cross


def split(group, turned):
    low, high = turned[:, :HALF], turned[:, HALF:]
    return jnp.where(group == 0, low, high), jnp.where(group == 0, high, low)


def focal_kernel(
    group_ref, pieces_ref, table_ref, keep_ref, first_ref, second_ref, gram_ref
):
    real = jnp.zeros((STACK, STACK), jnp.float32)
    cross = jnp.zeros((STACK, STACK), jnp.float32)
    for i in range(COLS):
        focal = focal_column(pieces_ref, table_ref, i)
        turned = [focal[part].T for part in range(2)]
        for part in range(2):
            at = 2 * i + part
            keep_ref[at], sent = split(group_ref[0], turned[part])
            if at < FIRST:
                first_ref[at] = sent
            else:
                second_ref[at - FIRST] = sent
        real, cross = add_gram(focal, turned, real, cross)
    imag = cross - cross.T
    row = lax.broadcasted_iota(jnp.int32, (STACK, STACK), 0)
    column = lax.broadcasted_iota(jnp.int32, (STACK, STACK), 1)
    packed = jnp.where(row <= column, real, imag)
    for q in range(4):
        top, left = (q // 2) * 128, (q % 2) * 128
        gram_ref[pl.ds(q, 128, stride=4), :] = packed[top : top + 128, left : left + 128]


def total_kernel(parts_ref, out_ref):
    total = jnp.sum(parts_ref[...].reshape(DEVICES // 2, 8, 128), axis=0)
    total = total[:4] + total[4:]
    twice = jnp.concatenate([total, total], axis=0)
    out_ref[...] = jnp.broadcast_to(twice[None], (DEVICES // 2, 8, 128)).reshape(4 * DEVICES, 128)


def power_kernel(gram_ref, start_ref, left_ref, scale_ref, power_ref):
    quads = [gram_ref[pl.ds(q, 128, stride=4), :] for q in range(4)]
    packed = jnp.concatenate(
        [jnp.concatenate(quads[:2], axis=1), jnp.concatenate(quads[2:], axis=1)], axis=0
    )
    turned = packed.T
    row = lax.broadcasted_iota(jnp.int32, (STACK, STACK), 0)
    column = lax.broadcasted_iota(jnp.int32, (STACK, STACK), 1)
    gram_re = jnp.where(row <= column, packed, turned)
    gram_im = jnp.where(row > column, packed, jnp.where(row == column, 0.0, -turned))
    gram = jnp.concatenate([gram_re, gram_im], axis=0)

    def pieces(value):
        first = value.astype(jnp.bfloat16)
        rest = value - first.astype(jnp.float32)
        second = rest.astype(jnp.bfloat16)
        return first, second, (rest - second.astype(jnp.float32)).astype(jnp.bfloat16)

    grams = pieces(gram)
    left = jnp.concatenate([grams[k] for k in (0, 1, 2, 0, 1, 0)], axis=1)

    def apply(re, im):
        both = jnp.concatenate([re, im], axis=1)
        if both.dtype == jnp.bfloat16:
            right = jnp.concatenate([both] * 3, axis=0)
        else:
            right = pieces(both)
            right = jnp.concatenate([right[k] for k in (0, 0, 0, 1, 1, 2)], axis=0)
        both = jnp.dot(left[:, : right.shape[0]], right, preferred_element_type=jnp.float32)
        return (
            both[:STACK, :RANK] - both[STACK:, RANK:],
            both[:STACK, RANK:] + both[STACK:, :RANK],
        )

    basis_re, basis_im = start_ref[0], start_ref[1]
    for _ in range(STEPS):
        image_re, image_im = apply(basis_re, basis_im)
        norm = jnp.sqrt(
            jnp.sum(image_re * image_re + image_im * image_im, axis=0, keepdims=True) + 1e-06
        )
        basis_re = image_re / norm
        basis_im = image_im / norm
    rounded_re = basis_re.astype(jnp.bfloat16)
    rounded_im = basis_im.astype(jnp.bfloat16)
    image_re, image_im = apply(rounded_re, rounded_im)
    rounded_re = rounded_re.astype(jnp.float32)
    rounded_im = rounded_im.astype(jnp.float32)
    energy = jnp.sum(rounded_re * image_re + rounded_im * image_im, axis=0, keepdims=True)
    trace = jnp.sum(jnp.where(row == column, packed, 0.0))
    power_ref[...] = energy * STACK / trace
    inverse = lax.rsqrt(energy / (NROW * NCOL) + 1e-06)
    scale_ref[...] = jnp.broadcast_to(inverse, (RANK, RANK)).T
    turned_re = rounded_re.T.astype(jnp.bfloat16)
    turned_im = rounded_im.T.astype(jnp.bfloat16)
    left_ref[:RANK, :STACK] = turned_re
    left_ref[:RANK, STACK:] = -turned_im
    left_ref[RANK:, :STACK] = turned_im
    left_ref[RANK:, STACK:] = turned_re


def modes_kernel(
    group_ref, left_ref, scale_ref, kept_ref, first_ref, second_ref, out_hbm,
       wide_ref, out_ref, out_sem,
):
    group = group_ref[0]
    left = left_ref[...]
    scale = scale_ref[...]
    sources = (
        [kept_ref[at] for at in range(2 * COLS)],
        [first_ref[at] for at in range(FIRST)]
        + [second_ref[at] for at in range(2 * COLS - FIRST)],
    )
    for source in range(2):
        first = jnp.where(group == source, 0, COLS)
        for i in range(COLS):
            focal = jnp.concatenate(sources[source][2 * i : 2 * i + 2], axis=0)
            mode = jnp.dot(left, focal, preferred_element_type=jnp.float32)
            for part in range(2):
                for lane in range(HALF // 128):
                    rows = pl.ds(
                        (part * 2 + lane) * WIDE + first + i, RANK, stride=GROUPS * COLS
                    )
                    wide_ref[rows, :] = (
                        mode[part * RANK : (part + 1) * RANK, lane * 128 : (lane + 1) * 128] * scale
                    )
    copies = []
    for part in range(2):
        for lane in range(HALF // 128):
            at = (part * 2 + lane) * WIDE
            out_ref[part, :, :, lane * 128 : (lane + 1) * 128] = (
                wide_ref[at : at + WIDE, :].reshape(RANK, GROUPS * COLS, 128).astype(jnp.bfloat16)
            )
        copies.append(pltpu.make_async_copy(out_ref.at[part], out_hbm.at[part], out_sem.at[part]))
        copies[-1].start()
    for copy in copies:
        copy.wait()


VMEM = pl.BlockSpec(memory_space=pltpu.VMEM)
HBM = pl.BlockSpec(memory_space=pltpu.HBM)
SMEM = pl.BlockSpec(memory_space=pltpu.SMEM)


def params(mib):
    return pltpu.CompilerParams(vmem_limit_bytes=mib * 1024 * 1024)


def local(fields, lens_phase, occupancy, focus_scale, assignment, start_basis):
    group = lax.axis_index("grp").astype(jnp.int32).reshape(1)
    column_table = jnp.asarray(column_tables())
    across = pl.pallas_call(
        spectra_kernel,
        out_shape=jax.ShapeDtypeStruct((DEVICES, COLS, 2 * ROWS, SLOTS), jnp.bfloat16),
        in_specs=[SMEM] + [HBM] * 6,
        out_specs=VMEM,
        scratch_shapes=[
            pltpu.SMEM((STACK,), jnp.int32),
            pltpu.SMEM((STACK,), jnp.float32),
            pltpu.SMEM((STACK,), jnp.float32),
            pltpu.VMEM((2, SLOTS, ROWS, NCOL), jnp.bfloat16),
            pltpu.VMEM((ROWS, NCOL), jnp.float32),
            pltpu.VMEM((2, NCOL, NCOL), jnp.bfloat16),
            pltpu.VMEM((BASES, 2, ROWS, NCOL), jnp.float32),
            pltpu.VMEM((NCOL // 128 * ROWS * SLOTS, 128), jnp.float32),
            pltpu.VMEM((NCOL // 128 * ROWS * SLOTS, 128), jnp.float32),
            pltpu.VMEM((2 * ROWS * PLANE, SLOTS), jnp.float32),
            pltpu.SemaphoreType.DMA((4,)),
            pltpu.SemaphoreType.DMA((2, CHUNKS)),
            pltpu.SemaphoreType.DMA((2,)),
        ],
        compiler_params=params(24),
        name="spectra",
    )(
        group,
        *(
            pltpu.with_memory_space_constraint(array, pltpu.HBM)
            for array in (
                assignment, occupancy, focus_scale, fields[0], lens_phase, column_table
            )
        ),
    )
    pieces = lax.all_to_all(across, AXES, 0, 0, tiled=True)
    pieces = pieces.reshape(DEVICES, COLS, 2, ROWS, SLOTS)


    def focal_shape(count):
        return jax.ShapeDtypeStruct((count, STACK, HALF), jnp.bfloat16)

    kept, swap_first, swap_second, gram = pl.pallas_call(
        focal_kernel,
        out_shape=(
            focal_shape(2 * COLS),
            focal_shape(FIRST),
            focal_shape(2 * COLS - FIRST),
            jax.ShapeDtypeStruct((4 * DEVICES, 128), jnp.float32),
        ),
        in_specs=[SMEM] + [VMEM] * 2,
        out_specs=(VMEM,) * 4,
        compiler_params=params(12),
        name="focal",
    )(group, pieces, jnp.asarray(row_tables()))
    swap_first = lax.ppermute(swap_first, "grp", [(0, 1), (1, 0)])
    swap_second = lax.ppermute(swap_second, "grp", [(0, 1), (1, 0)])
    parts = lax.all_to_all(gram.reshape(DEVICES, 4, 128), AXES, 0, 0, tiled=True)
    total = pl.pallas_call(
        total_kernel,
        out_shape=jax.ShapeDtypeStruct((4 * DEVICES, 128), jnp.float32),
        in_specs=[VMEM],
        out_specs=VMEM,
        compiler_params=params(4),
        name="total",
    )(parts.reshape(4 * DEVICES, 128))
    whole = lax.all_to_all(total.reshape(DEVICES, 4, 128), AXES, 0, 0, tiled=True)
    left, scale, power = pl.pallas_call(
        power_kernel,
        out_shape=(
            jax.ShapeDtypeStruct((2 * RANK, 2 * STACK), jnp.bfloat16),
            jax.ShapeDtypeStruct((RANK, RANK), jnp.float32),
            jax.ShapeDtypeStruct((1, RANK), jnp.float32),
        ),
        in_specs=[VMEM] * 2,
        out_specs=(VMEM,) * 3,
        compiler_params=params(12),
        name="power",
    )(whole.reshape(4 * DEVICES, 128), start_basis)
    coherent_modes = pl.pallas_call(
        modes_kernel,
        out_shape=jax.ShapeDtypeStruct((2, RANK, GROUPS * COLS, HALF), jnp.bfloat16),
        in_specs=[SMEM] + [VMEM] * 5,
        out_specs=HBM,
        scratch_shapes=[
            pltpu.VMEM((2 * HALF // 128 * WIDE, 128), jnp.float32),
            pltpu.VMEM((2, RANK, GROUPS * COLS, HALF), jnp.bfloat16),
            pltpu.SemaphoreType.DMA((2,)),
        ],
        compiler_params=params(16),
        name="modes",
    )(group, left, scale, kept, swap_first, swap_second)
    return coherent_modes, power.reshape(RANK)


def solution(mesh):
    in_specs = (P("grp", None, None, "pix", None), P("pix", None), P(), P(), P(), P())
    out_specs = (P(None, None, "pix", "grp"), P())

    return jax.shard_map(local, mesh=mesh, in_specs=in_specs, out_specs=out_specs, check_vma=False)
```

```python
import math

import jax
import jax.numpy as jnp
import numpy as np
from jax import lax
from jax.experimental import pallas as pl
from jax.experimental.pallas import tpu as pltpu
from jax.sharding import PartitionSpec as P

NROW = 512
NCOL = 512
STEPS = 2
GROUPS = 2
PIX = 64
DEVICES = GROUPS * PIX
SLOTS = 128
STACK = GROUPS * SLOTS
RANK = 128
ROWS = NROW // PIX
COLS = NCOL // DEVICES
HALF = NROW // GROUPS
WIDE = RANK * GROUPS * COLS
FIRST = 3
SENDS = 4
CHUNKS = 2
CHUNK = SLOTS // CHUNKS
PLANE = DEVICES * COLS + 1
AXES = ("grp", "pix")

LENS = 3.140625
SCALE_LOW, SCALE_HIGH = 0.5, 1.5
STEP = 0.125
BASES = int((SCALE_HIGH - SCALE_LOW) / STEP) + 1


def fit(function, terms, limit):
    nodes = np.cos(np.pi * (np.arange(400) + 0.5) / 400)
    square = (nodes + 1.0) * 0.5 * (limit * 1.001) ** 2
    powers = np.stack([square**k for k in range(terms)], axis=1)
    return [float(c) for c in np.linalg.lstsq(powers, function(np.sqrt(square)), rcond=None)[0]]


SIN_FIT = fit(lambda x: np.sin(x) / x, 6, 0.5 * SCALE_HIGH * LENS)
COS_FIT = fit(np.cos, 7, 0.5 * SCALE_HIGH * LENS)
SIN_REST = fit(lambda x: np.sin(x) / x, 3, 0.5 * STEP * LENS)
COS_REST = fit(np.cos, 3, 0.5 * STEP * LENS)


def tables(length):
    index = np.arange(length, dtype=np.int64)
    angle = (index[:, None] * index[None, :] % length).astype(np.float32) * np.float32(
        2.0 * math.pi / length
    )
    factor = np.float32(1.0 / math.sqrt(length))
    cosine = (np.cos(angle) * factor).astype(jnp.bfloat16)
    sine = (np.sin(angle) * factor).astype(jnp.bfloat16)
    return cosine, sine


def column_tables():
    i, g, p = np.meshgrid(
        np.arange(COLS), np.arange(GROUPS), np.arange(PIX // 2), indexing="ij"
    )
    order = (p * (GROUPS * COLS) + g * COLS + i).reshape(-1)
    pair = np.arange(0, NCOL, 256)[:, None]
    lane = np.arange(64)
    even = np.concatenate([pair + 2 * lane, pair + 128 + 2 * lane], axis=1).reshape(-1)
    odd = np.concatenate([pair + 129 + 2 * lane, pair + 1 + 2 * lane], axis=1).reshape(-1)
    cosine, sine = (table[order] for table in tables(NCOL))
    return np.stack(
        [
            np.block([[cosine[:, k], sine[:, k]], [-sine[:, k], cosine[:, k]]])
            for k in (even, odd)
        ]
    )


def row_tables():
    cosine, sine = (
        table[:HALF].reshape(HALF, PIX, ROWS // 2, 2).transpose(3, 0, 1, 2)
        for table in tables(NROW)
    )
    real = np.stack([cosine, sine], axis=3).reshape(2, HALF, NROW)
    imag = np.stack([-sine, cosine], axis=3).reshape(2, HALF, NROW)
    return np.concatenate([real, imag], axis=1)


def polynomial(square, coefficients):
    total = square * coefficients[-1] + coefficients[-2]
    for coefficient in coefficients[-3::-1]:
        total = total * square + coefficient
    return total


def spectra_kernel(
    group_ref, assign_hbm, occ_hbm, chrom_hbm, fields_hbm, lens_hbm, table_hbm, out_ref,
    assign_ref, occ_ref, chrom_ref, fields_ref, lens_ref, table_ref,
    base_ref, real_ref, imag_ref, wide_ref, small_sem, field_sem, table_sem,
):
    def chunk(part, c):
        slots = pl.ds(c * CHUNK, CHUNK)
        return pltpu.make_async_copy(
            fields_hbm.at[part, slots], fields_ref.at[part, slots], field_sem.at[part, c]
        )

    small = [
        pltpu.make_async_copy(source, target, small_sem.at[k])
        for k, (source, target) in enumerate(
            (
                (assign_hbm, assign_ref),
                (occ_hbm, occ_ref),
                (chrom_hbm, chrom_ref),
                (lens_hbm, lens_ref),
            )
        )
    ]
    large = [
        pltpu.make_async_copy(table_hbm.at[odd], table_ref.at[odd], table_sem.at[odd])
        for odd in range(2)
    ]
    for copy in small:
        copy.start()
    for c in range(CHUNKS):
        for part in range(2):
            chunk(part, c).start()
    for copy in large:
        copy.start()
    for copy in small:
        copy.wait()
    base = group_ref[0] * SLOTS

    def base_wave(k, carry):
        scale = 0.5 * (SCALE_LOW + STEP * k.astype(jnp.float32))
        for lane in range(NCOL // 128):
            cut = pl.ds(lane * 128, 128)
            half = lens_ref[:, cut] * scale
            square = half * half
            sine_half = half * polynomial(square, SIN_FIT)
            double = sine_half + sine_half
            base_ref[k, 0, :, cut] = 1.0 - double * sine_half
            base_ref[k, 1, :, cut] = double * polynomial(square, COS_FIT)
        return carry

    lax.fori_loop(0, BASES, base_wave, 0)

    def phase(m, carry):
        electron = assign_ref[base + m]
        amplitude = jnp.sqrt(jnp.full((ROWS, 128), occ_ref[electron], jnp.float32))
        chromatic = chrom_ref[electron]
        nearest = ((chromatic - SCALE_LOW) * (1.0 / STEP) + 0.5).astype(jnp.int32)
        nearest = jnp.clip(nearest, 0, BASES - 1)
        rest = chromatic - (SCALE_LOW + STEP * nearest.astype(jnp.float32))
        for lane in range(NCOL // 128):
            cut = pl.ds(lane * 128, 128)
            angle = lens_ref[:, cut] * rest
            square = angle * angle
            sine_rest = amplitude * (angle * polynomial(square, SIN_REST))
            cosine_rest = amplitude * polynomial(square, COS_REST)
            cosine_base = base_ref[nearest, 0, :, cut]
            sine_base = base_ref[nearest, 1, :, cut]
            cosine = cosine_base * cosine_rest - sine_base * sine_rest
            sine = sine_base * cosine_rest + cosine_base * sine_rest
            field_re = fields_ref[0, m, :, cut].astype(jnp.float32)
            field_im = fields_ref[1, m, :, cut].astype(jnp.float32)
            rows = pl.ds(pl.multiple_of(lane * ROWS * SLOTS + m * ROWS, ROWS), ROWS)
            real_ref[rows, :] = field_re * cosine - field_im * sine
            imag_ref[rows, :] = field_re * sine + field_im * cosine
        return carry

    for c in range(CHUNKS):
        for part in range(2):
            chunk(part, c).wait()
        lax.fori_loop(c * CHUNK, (c + 1) * CHUNK, phase, 0, unroll=16)
    for copy in large:
        copy.wait()
    lane = lax.broadcasted_iota(jnp.int32, (SLOTS, 128), 1)
    evens_first = 2 * (lane % 64) + lane // 64
    odds_first = 2 * (lane % 64) + 1 - lane // 64

    def parts(ref, j):
        even, odd = [], []
        for tile in range(0, NCOL // 128, 2):
            left, right = (
                ref[pl.ds((tile + k) * ROWS * SLOTS + j, SLOTS, stride=ROWS), :] for k in range(2)
            )
            left = jnp.take_along_axis(left, evens_first, axis=1)
            right = jnp.take_along_axis(right, odds_first, axis=1)
            even.append(jnp.where(lane < 64, left, right))
            odd.append(jnp.where(lane < 64, right, left))
        return even, odd

    contract = (((1,), (1,)), ((), ()))
    for j in range(0, ROWS, 2):
        waves = [[], []]
        for q in range(2):
            real, imag = parts(real_ref, j + q), parts(imag_ref, j + q)
            for odd in range(2):
                waves[odd].append(jnp.concatenate(real[odd] + imag[odd], axis=1))
        even, odd = (
            lax.dot_general(
                table_ref[k],
                jnp.concatenate(waves[k], axis=0).astype(jnp.bfloat16),
                contract,
                preferred_element_type=jnp.float32,
            )
            for k in range(2)
        )
        for half, across in ((0, even + odd), (1, even - odd)):
            for q in range(2):
                for part in range(2):
                    for block in range(COLS * GROUPS):
                        i, g = block // GROUPS, block % GROUPS
                        device = g * PIX + half * (PIX // 2)
                        at = q * ROWS + part * (ROWS // 2) + j // 2
                        row = part * (NCOL // 2) + block * (PIX // 2)
                        wide_ref[pl.ds(at * PLANE + i * DEVICES + device, PIX // 2), :] = across[
                            row : row + PIX // 2, q * SLOTS : (q + 1) * SLOTS
                        ]
    for i in range(COLS):

        def gather(d, carry):
            rows = wide_ref[pl.ds(i * DEVICES + d, 2 * ROWS, stride=PLANE), :]
            out_ref[d, i] = rows.astype(jnp.bfloat16)
            return carry

        lax.fori_loop(0, DEVICES, gather, 0, unroll=DEVICES)


def focal_column(pieces_ref, table_ref, i):
    halves = []
    for odd in range(2):
        wave = jnp.concatenate(
            [
                pieces_ref[g * PIX : (g + 1) * PIX, i, odd].reshape(NROW, SLOTS)
                for g in range(GROUPS)
            ],
            axis=1,
        )
        halves.append(jnp.dot(table_ref[odd], wave, preferred_element_type=jnp.float32))
    low = (halves[0] + halves[1]).astype(jnp.bfloat16)
    high = (halves[0] - halves[1]).astype(jnp.bfloat16)
    return [
        jnp.concatenate([half[part * HALF : (part + 1) * HALF] for half in (low, high)], axis=0)
        for part in range(2)
    ]


def add_gram(focal, turned, real, cross):
    real += jnp.dot(turned[0], focal[0], preferred_element_type=jnp.float32)
    real += jnp.dot(turned[1], focal[1], preferred_element_type=jnp.float32)
    cross += jnp.dot(turned[0], focal[1], preferred_element_type=jnp.float32)
    return real, cross


def split(group, turned):
    low, high = turned[:, :HALF], turned[:, HALF:]
    return jnp.where(group == 0, low, high), jnp.where(group == 0, high, low)


def focal_kernel(
    group_ref, pieces_ref, table_ref, keep_ref, first_ref, second_ref, gram_ref
):
    real = jnp.zeros((STACK, STACK), jnp.float32)
    cross = jnp.zeros((STACK, STACK), jnp.float32)
    for i in range(COLS):
        focal = focal_column(pieces_ref, table_ref, i)
        turned = [focal[part].T for part in range(2)]
        for part in range(2):
            at = 2 * i + part
            keep_ref[at], sent = split(group_ref[0], turned[part])
            if at < FIRST:
                first_ref[at] = sent
            else:
                second_ref[at - FIRST] = sent
        real, cross = add_gram(focal, turned, real, cross)
    imag = cross - cross.T
    row = lax.broadcasted_iota(jnp.int32, (STACK, STACK), 0)
    column = lax.broadcasted_iota(jnp.int32, (STACK, STACK), 1)
    packed = jnp.where(row <= column, real, imag)
    for q in range(4):
        top, left = (q // 2) * 128, (q % 2) * 128
        gram_ref[pl.ds(q, 128, stride=4), :] = packed[top : top + 128, left : left + 128]


def total_kernel(parts_ref, out_ref):
    total = jnp.sum(parts_ref[...].reshape(DEVICES // 2, 8, 128), axis=0)
    total = total[:4] + total[4:]
    twice = jnp.concatenate([total, total], axis=0)
    out_ref[...] = jnp.broadcast_to(twice[None], (DEVICES // 2, 8, 128)).reshape(4 * DEVICES, 128)


def power_kernel(gram_ref, start_ref, left_ref, scale_ref, power_ref):
    quads = [gram_ref[pl.ds(q, 128, stride=4), :] for q in range(4)]
    packed = jnp.concatenate(
        [jnp.concatenate(quads[:2], axis=1), jnp.concatenate(quads[2:], axis=1)], axis=0
    )
    turned = packed.T
    row = lax.broadcasted_iota(jnp.int32, (STACK, STACK), 0)
    column = lax.broadcasted_iota(jnp.int32, (STACK, STACK), 1)
    gram_re = jnp.where(row <= column, packed, turned)
    gram_im = jnp.where(row > column, packed, jnp.where(row == column, 0.0, -turned))
    gram = jnp.concatenate([gram_re, gram_im], axis=0)

    def pieces(value):
        first = value.astype(jnp.bfloat16)
        rest = value - first.astype(jnp.float32)
        second = rest.astype(jnp.bfloat16)
        return first, second, (rest - second.astype(jnp.float32)).astype(jnp.bfloat16)

    grams = pieces(gram)
    left = jnp.concatenate([grams[k] for k in (0, 1, 2, 0, 1, 0)], axis=1)

    def apply(re, im):
        both = jnp.concatenate([re, im], axis=1)
        if both.dtype == jnp.bfloat16:
            right = jnp.concatenate([both] * 3, axis=0)
        else:
            right = pieces(both)
            right = jnp.concatenate([right[k] for k in (0, 0, 0, 1, 1, 2)], axis=0)
        both = jnp.dot(left[:, : right.shape[0]], right, preferred_element_type=jnp.float32)
        return (
            both[:STACK, :RANK] - both[STACK:, RANK:],
            both[:STACK, RANK:] + both[STACK:, :RANK],
        )

    basis_re, basis_im = start_ref[0], start_ref[1]
    for _ in range(STEPS):
        image_re, image_im = apply(basis_re, basis_im)
        norm = jnp.sqrt(
            jnp.sum(image_re * image_re + image_im * image_im, axis=0, keepdims=True) + 1e-06
        )
        inverse = 1.0 / norm
        basis_re = image_re * inverse
        basis_im = image_im * inverse
    rounded_re = basis_re.astype(jnp.bfloat16)
    rounded_im = basis_im.astype(jnp.bfloat16)
    image_re, image_im = apply(rounded_re, rounded_im)
    rounded_re = rounded_re.astype(jnp.float32)
    rounded_im = rounded_im.astype(jnp.float32)
    energy = jnp.sum(rounded_re * image_re + rounded_im * image_im, axis=0, keepdims=True)
    trace = jnp.sum(jnp.where(row == column, packed, 0.0))
    power_ref[...] = energy * STACK / trace
    inverse = lax.rsqrt(energy / (NROW * NCOL) + 1e-06)
    scale_ref[...] = jnp.broadcast_to(inverse, (RANK, RANK)).T
    turned_re = rounded_re.T.astype(jnp.bfloat16)
    turned_im = rounded_im.T.astype(jnp.bfloat16)
    left_ref[:RANK, :STACK] = turned_re
    left_ref[:RANK, STACK:] = -turned_im
    left_ref[RANK:, :STACK] = turned_im
    left_ref[RANK:, STACK:] = turned_re


def modes_kernel(
    group_ref, left_ref, scale_ref, kept_ref, first_ref, second_ref, out_hbm,
       wide_ref, out_ref, out_sem,
):
    group = group_ref[0]
    left = left_ref[...]
    scale = scale_ref[...]
    sources = (
        [kept_ref[at] for at in range(2 * COLS)],
        [first_ref[at] for at in range(FIRST)]
        + [second_ref[at] for at in range(2 * COLS - FIRST)],
    )
    for source in range(2):
        first = jnp.where(group == source, 0, COLS)
        for i in range(COLS):
            focal = jnp.concatenate(sources[source][2 * i : 2 * i + 2], axis=0)
            mode = jnp.dot(left, focal, preferred_element_type=jnp.float32)
            for part in range(2):
                for lane in range(HALF // 128):
                    rows = pl.ds(
                        (part * 2 + lane) * WIDE + first + i, RANK, stride=GROUPS * COLS
                    )
                    wide_ref[rows, :] = (
                        mode[part * RANK : (part + 1) * RANK, lane * 128 : (lane + 1) * 128] * scale
                    )
    copies = []
    for piece in range(2 * SENDS):
        part, modes = piece // SENDS, RANK // SENDS
        first = piece % SENDS * modes
        for lane in range(HALF // 128):
            at = (part * 2 + lane) * WIDE + first * GROUPS * COLS
            out_ref[part, first : first + modes, :, lane * 128 : (lane + 1) * 128] = (
                wide_ref[at : at + modes * GROUPS * COLS, :]
                .reshape(modes, GROUPS * COLS, 128)
                .astype(jnp.bfloat16)
            )
        rows = pl.ds(first, modes)
        copies.append(
            pltpu.make_async_copy(
                out_ref.at[part, rows], out_hbm.at[part, rows], out_sem.at[piece]
            )
        )
        copies[-1].start()
    for copy in copies:
        copy.wait()


VMEM = pl.BlockSpec(memory_space=pltpu.VMEM)
HBM = pl.BlockSpec(memory_space=pltpu.HBM)
SMEM = pl.BlockSpec(memory_space=pltpu.SMEM)


def params(mib):
    return pltpu.CompilerParams(vmem_limit_bytes=mib * 1024 * 1024)


def local(fields, lens_phase, occupancy, focus_scale, assignment, start_basis):
    group = lax.axis_index("grp").astype(jnp.int32).reshape(1)
    column_table = jnp.asarray(column_tables())
    across = pl.pallas_call(
        spectra_kernel,
        out_shape=jax.ShapeDtypeStruct((DEVICES, COLS, 2 * ROWS, SLOTS), jnp.bfloat16),
        in_specs=[SMEM] + [HBM] * 6,
        out_specs=VMEM,
        scratch_shapes=[
            pltpu.SMEM((STACK,), jnp.int32),
            pltpu.SMEM((STACK,), jnp.float32),
            pltpu.SMEM((STACK,), jnp.float32),
            pltpu.VMEM((2, SLOTS, ROWS, NCOL), jnp.bfloat16),
            pltpu.VMEM((ROWS, NCOL), jnp.float32),
            pltpu.VMEM((2, NCOL, NCOL), jnp.bfloat16),
            pltpu.VMEM((BASES, 2, ROWS, NCOL), jnp.float32),
            pltpu.VMEM((NCOL // 128 * ROWS * SLOTS, 128), jnp.float32),
            pltpu.VMEM((NCOL // 128 * ROWS * SLOTS, 128), jnp.float32),
            pltpu.VMEM((2 * ROWS * PLANE, SLOTS), jnp.float32),
            pltpu.SemaphoreType.DMA((4,)),
            pltpu.SemaphoreType.DMA((2, CHUNKS)),
            pltpu.SemaphoreType.DMA((2,)),
        ],
        compiler_params=params(24),
        name="spectra",
    )(
        group,
        *(
            pltpu.with_memory_space_constraint(array, pltpu.HBM)
            for array in (
                assignment, occupancy, focus_scale, fields[0], lens_phase, column_table
            )
        ),
    )
    pieces = lax.all_to_all(across, AXES, 0, 0, tiled=True)
    pieces = pieces.reshape(DEVICES, COLS, 2, ROWS, SLOTS)


    def focal_shape(count):
        return jax.ShapeDtypeStruct((count, STACK, HALF), jnp.bfloat16)

    kept, swap_first, swap_second, gram = pl.pallas_call(
        focal_kernel,
        out_shape=(
            focal_shape(2 * COLS),
            focal_shape(FIRST),
            focal_shape(2 * COLS - FIRST),
            jax.ShapeDtypeStruct((4 * DEVICES, 128), jnp.float32),
        ),
        in_specs=[SMEM] + [VMEM] * 2,
        out_specs=(VMEM,) * 4,
        compiler_params=params(12),
        name="focal",
    )(group, pieces, jnp.asarray(row_tables()))
    swap_first = lax.ppermute(swap_first, "grp", [(0, 1), (1, 0)])
    swap_second = lax.ppermute(swap_second, "grp", [(0, 1), (1, 0)])
    parts = lax.all_to_all(gram.reshape(DEVICES, 4, 128), AXES, 0, 0, tiled=True)
    total = pl.pallas_call(
        total_kernel,
        out_shape=jax.ShapeDtypeStruct((4 * DEVICES, 128), jnp.float32),
        in_specs=[VMEM],
        out_specs=VMEM,
        compiler_params=params(4),
        name="total",
    )(parts.reshape(4 * DEVICES, 128))
    whole = lax.all_to_all(total.reshape(DEVICES, 4, 128), AXES, 0, 0, tiled=True)
    left, scale, power = pl.pallas_call(
        power_kernel,
        out_shape=(
            jax.ShapeDtypeStruct((2 * RANK, 2 * STACK), jnp.bfloat16),
            jax.ShapeDtypeStruct((RANK, RANK), jnp.float32),
            jax.ShapeDtypeStruct((1, RANK), jnp.float32),
        ),
        in_specs=[VMEM] * 2,
        out_specs=(VMEM,) * 3,
        compiler_params=params(12),
        name="power",
    )(whole.reshape(4 * DEVICES, 128), start_basis)
    coherent_modes = pl.pallas_call(
        modes_kernel,
        out_shape=jax.ShapeDtypeStruct((2, RANK, GROUPS * COLS, HALF), jnp.bfloat16),
        in_specs=[SMEM] + [VMEM] * 5,
        out_specs=HBM,
        scratch_shapes=[
            pltpu.VMEM((2 * HALF // 128 * WIDE, 128), jnp.float32),
            pltpu.VMEM((2, RANK, GROUPS * COLS, HALF), jnp.bfloat16),
            pltpu.SemaphoreType.DMA((2 * SENDS,)),
        ],
        compiler_params=params(16),
        name="modes",
    )(group, left, scale, kept, swap_first, swap_second)
    return coherent_modes, power.reshape(RANK)


def solution(mesh):
    in_specs = (P("grp", None, None, "pix", None), P("pix", None), P(), P(), P(), P())
    out_specs = (P(None, None, "pix", "grp"), P())

    return jax.shard_map(local, mesh=mesh, in_specs=in_specs, out_specs=out_specs, check_vma=False)
```

```python
import math

import jax
import jax.numpy as jnp
import numpy as np
from jax import lax
from jax.experimental import pallas as pl
from jax.experimental.pallas import tpu as pltpu
from jax.sharding import PartitionSpec as P

NROW = 512
NCOL = 512
STEPS = 2
GROUPS = 2
PIX = 64
DEVICES = GROUPS * PIX
SLOTS = 128
STACK = GROUPS * SLOTS
RANK = 128
ROWS = NROW // PIX
COLS = NCOL // DEVICES
HALF = NROW // GROUPS
PITCH = RANK + 1
WIDE = PITCH * GROUPS * COLS
FIRST = 3
CHUNKS = 4
CHUNK = SLOTS // CHUNKS
PLANE = DEVICES * COLS + 1
AXES = ("grp", "pix")

LENS = 3.140625
SCALE_LOW, SCALE_HIGH = 0.5, 1.5
STEP = 0.125
BASES = int((SCALE_HIGH - SCALE_LOW) / STEP) + 1


def fit(function, terms, limit):
    nodes = np.cos(np.pi * (np.arange(400) + 0.5) / 400)
    square = (nodes + 1.0) * 0.5 * (limit * 1.001) ** 2
    powers = np.stack([square**k for k in range(terms)], axis=1)
    return [float(c) for c in np.linalg.lstsq(powers, function(np.sqrt(square)), rcond=None)[0]]


SIN_FIT = fit(lambda x: np.sin(x) / x, 6, 0.5 * SCALE_HIGH * LENS)
COS_FIT = fit(np.cos, 7, 0.5 * SCALE_HIGH * LENS)
SIN_REST = fit(lambda x: np.sin(x) / x, 3, 0.5 * STEP * LENS)
COS_REST = fit(np.cos, 3, 0.5 * STEP * LENS)


def tables(length):
    index = np.arange(length, dtype=np.int64)
    angle = (index[:, None] * index[None, :] % length).astype(np.float32) * np.float32(
        2.0 * math.pi / length
    )
    factor = np.float32(1.0 / math.sqrt(length))
    cosine = (np.cos(angle) * factor).astype(jnp.bfloat16)
    sine = (np.sin(angle) * factor).astype(jnp.bfloat16)
    return cosine, sine


def column_tables():
    i, g, p = np.meshgrid(
        np.arange(COLS), np.arange(GROUPS), np.arange(PIX // 2), indexing="ij"
    )
    order = (p * (GROUPS * COLS) + g * COLS + i).reshape(-1)
    pair = np.arange(0, NCOL, 256)[:, None]
    lane = np.arange(64)
    even = np.concatenate([pair + 2 * lane, pair + 128 + 2 * lane], axis=1).reshape(-1)
    odd = np.concatenate([pair + 129 + 2 * lane, pair + 1 + 2 * lane], axis=1).reshape(-1)
    cosine, sine = (table[order] for table in tables(NCOL))
    return np.stack(
        [
            np.block([[cosine[:, k], sine[:, k]], [-sine[:, k], cosine[:, k]]])
            for k in (even, odd)
        ]
    )


def row_tables():
    cosine, sine = (
        table[:HALF].reshape(HALF, PIX, ROWS // 2, 2).transpose(3, 0, 1, 2)
        for table in tables(NROW)
    )
    real = np.stack([cosine, sine], axis=3).reshape(2, HALF, NROW)
    imag = np.stack([-sine, cosine], axis=3).reshape(2, HALF, NROW)
    return np.concatenate([real, imag], axis=1)


def polynomial(square, coefficients):
    total = square * coefficients[-1] + coefficients[-2]
    for coefficient in coefficients[-3::-1]:
        total = total * square + coefficient
    return total


def spectra_kernel(
    group_ref, assign_hbm, occ_hbm, chrom_hbm, fields_hbm, lens_hbm, table_hbm, out_ref,
    assign_ref, occ_ref, chrom_ref, fields_ref, lens_ref, table_ref,
    base_ref, real_ref, imag_ref, wide_ref, small_sem, field_sem, table_sem,
):
    def chunk(part, c):
        slots = pl.ds(c * CHUNK, CHUNK)
        return pltpu.make_async_copy(
            fields_hbm.at[part, slots], fields_ref.at[part, slots], field_sem.at[part, c]
        )

    small = [
        pltpu.make_async_copy(source, target, small_sem.at[k])
        for k, (source, target) in enumerate(
            (
                (assign_hbm, assign_ref),
                (occ_hbm, occ_ref),
                (chrom_hbm, chrom_ref),
                (lens_hbm, lens_ref),
            )
        )
    ]
    large = [
        pltpu.make_async_copy(table_hbm.at[odd], table_ref.at[odd], table_sem.at[odd])
        for odd in range(2)
    ]
    for copy in small:
        copy.start()
    for c in range(CHUNKS):
        for part in range(2):
            chunk(part, c).start()
    for copy in large:
        copy.start()
    for copy in small:
        copy.wait()
    base = group_ref[0] * SLOTS

    def base_wave(k, carry):
        scale = 0.5 * (SCALE_LOW + STEP * k.astype(jnp.float32))
        for lane in range(NCOL // 128):
            cut = pl.ds(lane * 128, 128)
            half = lens_ref[:, cut] * scale
            square = half * half
            sine_half = half * polynomial(square, SIN_FIT)
            double = sine_half + sine_half
            base_ref[k, 0, :, cut] = 1.0 - double * sine_half
            base_ref[k, 1, :, cut] = double * polynomial(square, COS_FIT)
        return carry

    lax.fori_loop(0, BASES, base_wave, 0)

    def phase(m, carry):
        electron = assign_ref[base + m]
        amplitude = jnp.sqrt(jnp.full((ROWS, 128), occ_ref[electron], jnp.float32))
        chromatic = chrom_ref[electron]
        nearest = ((chromatic - SCALE_LOW) * (1.0 / STEP) + 0.5).astype(jnp.int32)
        nearest = jnp.clip(nearest, 0, BASES - 1)
        rest = chromatic - (SCALE_LOW + STEP * nearest.astype(jnp.float32))
        for lane in range(NCOL // 128):
            cut = pl.ds(lane * 128, 128)
            angle = lens_ref[:, cut] * rest
            square = angle * angle
            sine_rest = amplitude * (angle * polynomial(square, SIN_REST))
            cosine_rest = amplitude * polynomial(square, COS_REST)
            cosine_base = base_ref[nearest, 0, :, cut]
            sine_base = base_ref[nearest, 1, :, cut]
            cosine = cosine_base * cosine_rest - sine_base * sine_rest
            sine = sine_base * cosine_rest + cosine_base * sine_rest
            field_re = fields_ref[0, m, :, cut].astype(jnp.float32)
            field_im = fields_ref[1, m, :, cut].astype(jnp.float32)
            rows = pl.ds(pl.multiple_of(lane * ROWS * SLOTS + m * ROWS, ROWS), ROWS)
            real_ref[rows, :] = field_re * cosine - field_im * sine
            imag_ref[rows, :] = field_re * sine + field_im * cosine
        return carry

    for c in range(CHUNKS):
        for part in range(2):
            chunk(part, c).wait()
        lax.fori_loop(c * CHUNK, (c + 1) * CHUNK, phase, 0, unroll=16)
    for copy in large:
        copy.wait()
    lane = lax.broadcasted_iota(jnp.int32, (SLOTS, 128), 1)
    evens_first = 2 * (lane % 64) + lane // 64
    odds_first = 2 * (lane % 64) + 1 - lane // 64

    def parts(ref, j):
        even, odd = [], []
        for tile in range(0, NCOL // 128, 2):
            left, right = (
                ref[pl.ds((tile + k) * ROWS * SLOTS + j, SLOTS, stride=ROWS), :] for k in range(2)
            )
            left = jnp.take_along_axis(left, evens_first, axis=1)
            right = jnp.take_along_axis(right, odds_first, axis=1)
            even.append(jnp.where(lane < 64, left, right))
            odd.append(jnp.where(lane < 64, right, left))
        return even, odd

    contract = (((1,), (1,)), ((), ()))
    for j in range(0, ROWS, 2):
        waves = [[], []]
        for q in range(2):
            real, imag = parts(real_ref, j + q), parts(imag_ref, j + q)
            for odd in range(2):
                waves[odd].append(jnp.concatenate(real[odd] + imag[odd], axis=1))
        even, odd = (
            lax.dot_general(
                table_ref[k],
                jnp.concatenate(waves[k], axis=0).astype(jnp.bfloat16),
                contract,
                preferred_element_type=jnp.float32,
            )
            for k in range(2)
        )
        for half, across in ((0, even + odd), (1, even - odd)):
            for q in range(2):
                for part in range(2):
                    for block in range(COLS * GROUPS):
                        i, g = block // GROUPS, block % GROUPS
                        device = g * PIX + half * (PIX // 2)
                        at = q * ROWS + part * (ROWS // 2) + j // 2
                        row = part * (NCOL // 2) + block * (PIX // 2)
                        wide_ref[pl.ds(at * PLANE + i * DEVICES + device, PIX // 2), :] = across[
                            row : row + PIX // 2, q * SLOTS : (q + 1) * SLOTS
                        ]
    for i in range(COLS):

        def gather(d, carry):
            rows = wide_ref[pl.ds(i * DEVICES + d, 2 * ROWS, stride=PLANE), :]
            out_ref[d, i] = rows.astype(jnp.bfloat16)
            return carry

        lax.fori_loop(0, DEVICES, gather, 0, unroll=DEVICES)


def focal_column(pieces_ref, table_ref, i):
    halves = []
    for odd in range(2):
        wave = jnp.concatenate(
            [
                pieces_ref[g * PIX : (g + 1) * PIX, i, odd].reshape(NROW, SLOTS)
                for g in range(GROUPS)
            ],
            axis=1,
        )
        halves.append(jnp.dot(table_ref[odd], wave, preferred_element_type=jnp.float32))
    low = (halves[0] + halves[1]).astype(jnp.bfloat16)
    high = (halves[0] - halves[1]).astype(jnp.bfloat16)
    return [
        jnp.concatenate([half[part * HALF : (part + 1) * HALF] for half in (low, high)], axis=0)
        for part in range(2)
    ]


def add_gram(focal, turned, real, cross):
    real += jnp.dot(turned[0], focal[0], preferred_element_type=jnp.float32)
    real += jnp.dot(turned[1], focal[1], preferred_element_type=jnp.float32)
    cross += jnp.dot(turned[0], focal[1], preferred_element_type=jnp.float32)
    return real, cross


def split(group, turned):
    low, high = turned[:, :HALF], turned[:, HALF:]
    return jnp.where(group == 0, low, high), jnp.where(group == 0, high, low)


def focal_kernel(
    group_ref, pieces_ref, table_ref, keep_ref, first_ref, second_ref, gram_ref
):
    real = jnp.zeros((STACK, STACK), jnp.float32)
    cross = jnp.zeros((STACK, STACK), jnp.float32)
    for i in range(COLS):
        focal = focal_column(pieces_ref, table_ref, i)
        turned = [focal[part].T for part in range(2)]
        for part in range(2):
            at = 2 * i + part
            keep_ref[at], sent = split(group_ref[0], turned[part])
            if at < FIRST:
                first_ref[at] = sent
            else:
                second_ref[at - FIRST] = sent
        real, cross = add_gram(focal, turned, real, cross)
    imag = cross - cross.T
    row = lax.broadcasted_iota(jnp.int32, (STACK, STACK), 0)
    column = lax.broadcasted_iota(jnp.int32, (STACK, STACK), 1)
    packed = jnp.where(row <= column, real, imag)
    for q in range(4):
        top, left = (q // 2) * 128, (q % 2) * 128
        gram_ref[pl.ds(q, 128, stride=4), :] = packed[top : top + 128, left : left + 128]


def total_kernel(parts_ref, out_ref):
    total = jnp.sum(parts_ref[...].reshape(DEVICES // 2, 8, 128), axis=0)
    total = total[:4] + total[4:]
    twice = jnp.concatenate([total, total], axis=0)
    out_ref[...] = jnp.broadcast_to(twice[None], (DEVICES // 2, 8, 128)).reshape(4 * DEVICES, 128)


def power_kernel(gram_ref, start_ref, left_ref, scale_ref, power_ref):
    quads = [gram_ref[pl.ds(q, 128, stride=4), :] for q in range(4)]
    packed = jnp.concatenate(
        [jnp.concatenate(quads[:2], axis=1), jnp.concatenate(quads[2:], axis=1)], axis=0
    )
    turned = packed.T
    row = lax.broadcasted_iota(jnp.int32, (STACK, STACK), 0)
    column = lax.broadcasted_iota(jnp.int32, (STACK, STACK), 1)
    gram_re = jnp.where(row <= column, packed, turned)
    gram_im = jnp.where(row > column, packed, jnp.where(row == column, 0.0, -turned))
    gram = jnp.concatenate([gram_re, gram_im], axis=0)

    def pieces(value):
        first = value.astype(jnp.bfloat16)
        rest = value - first.astype(jnp.float32)
        second = rest.astype(jnp.bfloat16)
        return first, second, (rest - second.astype(jnp.float32)).astype(jnp.bfloat16)

    grams = pieces(gram)
    left = jnp.concatenate([grams[k] for k in (0, 1, 2, 0, 1, 0)], axis=1)

    def apply(re, im):
        both = jnp.concatenate([re, im], axis=1)
        if both.dtype == jnp.bfloat16:
            right = jnp.concatenate([both] * 3, axis=0)
        else:
            right = pieces(both)
            right = jnp.concatenate([right[k] for k in (0, 0, 0, 1, 1, 2)], axis=0)
        both = jnp.dot(left[:, : right.shape[0]], right, preferred_element_type=jnp.float32)
        return (
            both[:STACK, :RANK] - both[STACK:, RANK:],
            both[:STACK, RANK:] + both[STACK:, :RANK],
        )

    basis_re, basis_im = start_ref[0], start_ref[1]
    for _ in range(STEPS):
        image_re, image_im = apply(basis_re, basis_im)
        norm = jnp.sqrt(
            jnp.sum(image_re * image_re + image_im * image_im, axis=0, keepdims=True) + 1e-06
        )
        basis_re = image_re / norm
        basis_im = image_im / norm
    rounded_re = basis_re.astype(jnp.bfloat16)
    rounded_im = basis_im.astype(jnp.bfloat16)
    image_re, image_im = apply(rounded_re, rounded_im)
    rounded_re = rounded_re.astype(jnp.float32)
    rounded_im = rounded_im.astype(jnp.float32)
    energy = jnp.sum(rounded_re * image_re + rounded_im * image_im, axis=0, keepdims=True)
    trace = jnp.sum(jnp.where(row == column, packed, 0.0))
    power_ref[...] = energy * STACK / trace
    inverse = lax.rsqrt(energy / (NROW * NCOL) + 1e-06)
    scale_ref[...] = jnp.broadcast_to(inverse, (RANK, RANK)).T
    turned_re = rounded_re.T.astype(jnp.bfloat16)
    turned_im = rounded_im.T.astype(jnp.bfloat16)
    left_ref[:RANK, :STACK] = turned_re
    left_ref[:RANK, STACK:] = -turned_im
    left_ref[RANK:, :STACK] = turned_im
    left_ref[RANK:, STACK:] = turned_re


def modes_kernel(
    group_ref, left_ref, scale_ref, kept_ref, first_ref, second_ref, out_hbm,
       wide_ref, out_ref, out_sem,
):
    group = group_ref[0]
    left = left_ref[...]
    scale = scale_ref[...]
    sources = (
        [kept_ref[at] for at in range(2 * COLS)],
        [first_ref[at] for at in range(FIRST)]
        + [second_ref[at] for at in range(2 * COLS - FIRST)],
    )
    for source in range(2):
        first = jnp.where(group == source, 0, COLS)
        for i in range(COLS):
            focal = jnp.concatenate(sources[source][2 * i : 2 * i + 2], axis=0)
            mode = jnp.dot(left, focal, preferred_element_type=jnp.float32)
            for part in range(2):
                for lane in range(HALF // 128):
                    rows = pl.ds((part * 2 + lane) * WIDE + (first + i) * PITCH, RANK)
                    wide_ref[rows, :] = (
                        mode[part * RANK : (part + 1) * RANK, lane * 128 : (lane + 1) * 128] * scale
                    )
    copies = []
    for part in range(2):
        for lane in range(HALF // 128):
            at = (part * 2 + lane) * WIDE

            def gather(k, carry):
                rows = wide_ref[pl.ds(at + k, GROUPS * COLS, stride=PITCH), :]
                out_ref[part, k, :, lane * 128 : (lane + 1) * 128] = rows.astype(jnp.bfloat16)
                return carry

            lax.fori_loop(0, RANK, gather, 0, unroll=16)
        copies.append(pltpu.make_async_copy(out_ref.at[part], out_hbm.at[part], out_sem.at[part]))
        copies[-1].start()
    for copy in copies:
        copy.wait()


VMEM = pl.BlockSpec(memory_space=pltpu.VMEM)
HBM = pl.BlockSpec(memory_space=pltpu.HBM)
SMEM = pl.BlockSpec(memory_space=pltpu.SMEM)


def params(mib):
    return pltpu.CompilerParams(vmem_limit_bytes=mib * 1024 * 1024)


def local(fields, lens_phase, occupancy, focus_scale, assignment, start_basis):
    group = lax.axis_index("grp").astype(jnp.int32).reshape(1)
    column_table = jnp.asarray(column_tables())
    across = pl.pallas_call(
        spectra_kernel,
        out_shape=jax.ShapeDtypeStruct((DEVICES, COLS, 2 * ROWS, SLOTS), jnp.bfloat16),
        in_specs=[SMEM] + [HBM] * 6,
        out_specs=VMEM,
        scratch_shapes=[
            pltpu.SMEM((STACK,), jnp.int32),
            pltpu.SMEM((STACK,), jnp.float32),
            pltpu.SMEM((STACK,), jnp.float32),
            pltpu.VMEM((2, SLOTS, ROWS, NCOL), jnp.bfloat16),
            pltpu.VMEM((ROWS, NCOL), jnp.float32),
            pltpu.VMEM((2, NCOL, NCOL), jnp.bfloat16),
            pltpu.VMEM((BASES, 2, ROWS, NCOL), jnp.float32),
            pltpu.VMEM((NCOL // 128 * ROWS * SLOTS, 128), jnp.float32),
            pltpu.VMEM((NCOL // 128 * ROWS * SLOTS, 128), jnp.float32),
            pltpu.VMEM((2 * ROWS * PLANE, SLOTS), jnp.float32),
            pltpu.SemaphoreType.DMA((4,)),
            pltpu.SemaphoreType.DMA((2, CHUNKS)),
            pltpu.SemaphoreType.DMA((2,)),
        ],
        compiler_params=params(24),
        name="spectra",
    )(
        group,
        *(
            pltpu.with_memory_space_constraint(array, pltpu.HBM)
            for array in (
                assignment, occupancy, focus_scale, fields[0], lens_phase, column_table
            )
        ),
    )
    pieces = lax.all_to_all(across, AXES, 0, 0, tiled=True)
    pieces = pieces.reshape(DEVICES, COLS, 2, ROWS, SLOTS)


    def focal_shape(count):
        return jax.ShapeDtypeStruct((count, STACK, HALF), jnp.bfloat16)

    kept, swap_first, swap_second, gram = pl.pallas_call(
        focal_kernel,
        out_shape=(
            focal_shape(2 * COLS),
            focal_shape(FIRST),
            focal_shape(2 * COLS - FIRST),
            jax.ShapeDtypeStruct((4 * DEVICES, 128), jnp.float32),
        ),
        in_specs=[SMEM] + [VMEM] * 2,
        out_specs=(VMEM,) * 4,
        compiler_params=params(12),
        name="focal",
    )(group, pieces, jnp.asarray(row_tables()))
    swap_first = lax.ppermute(swap_first, "grp", [(0, 1), (1, 0)])
    swap_second = lax.ppermute(swap_second, "grp", [(0, 1), (1, 0)])
    parts = lax.all_to_all(gram.reshape(DEVICES, 4, 128), AXES, 0, 0, tiled=True)
    total = pl.pallas_call(
        total_kernel,
        out_shape=jax.ShapeDtypeStruct((4 * DEVICES, 128), jnp.float32),
        in_specs=[VMEM],
        out_specs=VMEM,
        compiler_params=params(4),
        name="total",
    )(parts.reshape(4 * DEVICES, 128))
    whole = lax.all_to_all(total.reshape(DEVICES, 4, 128), AXES, 0, 0, tiled=True)
    left, scale, power = pl.pallas_call(
        power_kernel,
        out_shape=(
            jax.ShapeDtypeStruct((2 * RANK, 2 * STACK), jnp.bfloat16),
            jax.ShapeDtypeStruct((RANK, RANK), jnp.float32),
            jax.ShapeDtypeStruct((1, RANK), jnp.float32),
        ),
        in_specs=[VMEM] * 2,
        out_specs=(VMEM,) * 3,
        compiler_params=params(12),
        name="power",
    )(whole.reshape(4 * DEVICES, 128), start_basis)
    coherent_modes = pl.pallas_call(
        modes_kernel,
        out_shape=jax.ShapeDtypeStruct((2, RANK, GROUPS * COLS, HALF), jnp.bfloat16),
        in_specs=[SMEM] + [VMEM] * 5,
        out_specs=HBM,
        scratch_shapes=[
            pltpu.VMEM((2 * HALF // 128 * WIDE, 128), jnp.float32),
            pltpu.VMEM((2, RANK, GROUPS * COLS, HALF), jnp.bfloat16),
            pltpu.SemaphoreType.DMA((2,)),
        ],
        compiler_params=params(16),
        name="modes",
    )(group, left, scale, kept, swap_first, swap_second)
    return coherent_modes, power.reshape(RANK)


def solution(mesh):
    in_specs = (P("grp", None, None, "pix", None), P("pix", None), P(), P(), P(), P())
    out_specs = (P(None, None, "pix", "grp"), P())

    return jax.shard_map(local, mesh=mesh, in_specs=in_specs, out_specs=out_specs, check_vma=False)
```
